128 devices in a mesh: req: 16 (over z, y), mlp: 8 (over x, core).
Axes of the slice: x: 4, y: 4, z: 4, core: 2. Of those that a mesh axis runs over, the one named last changes fastest.
Arguments:
- hidden: bfloat16 [8192, 3584], P('req', 'mlp'), may hold values from -6 to 6
- query_heads: bfloat16 [8192, 3584], P('req', 'mlp'), may hold values from -4 to 4
- key_heads: bfloat16 [8192, 3584], P('req', 'mlp'), may hold values from -4 to 4
- value_heads: bfloat16 [8192, 3584], P('req', 'mlp'), may hold values from -6 to 6
- segment_ids: int32 [8192], P('req'), may hold values from 0 to 63, never falling along the last dimension, each value on 1 to 1024 neighbouring positions
- page_table: int32 [16, 32], P('req'), may hold values from 0 to 31, each once within a row
- mamba_conv_input: bfloat16 [8192, 7168], P('req', 'mlp'), may hold values from -6 to 6
- mamba_output_gate: bfloat16 [8192, 7168], P('req', 'mlp'), may hold values from -6 to 6
- state_input_projection: bfloat16 [8192, 128], P('req'), may hold values from -6 to 6
- state_output_projection: bfloat16 [8192, 128], P('req'), may hold values from -6 to 6
- discrete_step_size: float32 [8192, 112], P('req', 'mlp'), may hold values from 0.24 to 100, as said below
- head_decay_rate: float32 [112], P('mlp'), may hold values from 0.00024414062 to 0.05, as said below
- skip_gain: float32 [112], P('mlp'), may hold values from 0.5 to 2
- mamba_gated_norm_gain: float32 [7168], P('mlp'), may hold values from 0.1 to 1.9
- attn_proj: bfloat16 [3584, 3584], P('mlp'), may hold values from -0.09375 to 0.09375
- mamba_output_projection: bfloat16 [7168, 3584], P('mlp'), may hold values from -0.0625 to 0.0625
- mlp_norm_gain: float32 [3584], replicated, may hold values from 0.1 to 1.9
- gate_proj: bfloat16 [3584, 7168], P('req', 'mlp'), may hold values from -0.09375 to 0.09375
- up_proj: bfloat16 [3584, 7168], P('req', 'mlp'), may hold values from -0.09375 to 0.09375
- down_proj: bfloat16 [7168, 3584], P('mlp', 'req'), may hold values from -0.0625 to 0.0625
- next_norm_gain: float32 [3584], P('mlp'), may hold values from 0.1 to 1.9
Outputs:
- new_hidden: bfloat16 [8192, 3584], P('req', 'mlp')
- next_normed: bfloat16 [8192, 3584], P('req', 'mlp')
- kv_cache: bfloat16 [2, 16, 512, 3584], P(None, 'mlp', 'req')
The draws below stay inside these ranges and needn't reach their ends.
Inputs may be any that keep to these rules, and one draw needn't show every extreme that they name: `segment_ids`: prompt ids never fall along the stream; a prompt has 1 to 1024 tokens and one has exactly 1024. `page_table`: each request group's row names every page of its pool once. `discrete_step_size`: Positive. `head_decay_rate`: Positive.
All inputs are finite; a program needn't handle non-finite values.
Results may differ from the reference program's by a relative error of at most 0.006.
Values may be sent and summed in bfloat16 or wider, within the bound.
No kernel may reach another device: no remote copies, remote signals or barrier semaphores. Data moves between devices by JAX's collectives and lax.ppermute only.
A program may use at most 128 MiB of HBM per device.

```python
import math
import jax
import jax.numpy as jnp
import numpy as np
from jax import lax

MODEL_WIDTH = 3584
HEADS_A = 16
HD = 224
MAMBA_HEAD_COUNT = 112
MAMBA_HEAD_SIZE = 64
STATE_SIZE = 64
STATE_GROUPS = 2
FF = 7168
PROMPT_SPAN = 512
REACH = 2
PAGE = 16
PACKED_LENGTH = 8192
MAXLEN = 1024
NSEG = 64
PAGES_DEV = 32
N_REQ = 16


def query_key_pair(master_seed_draw):
    first_key = jax.random.fold_in(master_seed_draw, 11)
    second_key = jax.random.fold_in(master_seed_draw, 12)
    array_shape = (PACKED_LENGTH, HEADS_A * HD)
    queries = jnp.clip(jax.random.normal(first_key, array_shape, jnp.float32), -4.0, 4.0)
    keys_drawn = jnp.clip(jax.random.normal(second_key, array_shape, jnp.float32), -4.0, 4.0)
    return (queries, keys_drawn)


def draw_query_heads(master_seed_draw, part):
    return query_key_pair(master_seed_draw)[0].astype(jnp.bfloat16)


def draw_key_heads(master_seed_draw, part):
    return query_key_pair(master_seed_draw)[1].astype(jnp.bfloat16)


def draw_discrete_step_size(master_seed_draw, part):
    level_key = jax.random.fold_in(master_seed_draw, 21)
    block_key = jax.random.fold_in(master_seed_draw, 22)
    flurry_seed_draw = jax.random.fold_in(master_seed_draw, 23)
    levels = jnp.exp(jax.random.uniform(level_key, (PACKED_LENGTH, MAMBA_HEAD_COUNT), jnp.float32, -0.7, 0.7))
    block_scale = jnp.exp(jax.random.uniform(block_key, (PACKED_LENGTH // PROMPT_SPAN, 1), jnp.float32, -0.7, 0.7))
    rescaled_amounts = (levels.reshape(PACKED_LENGTH // PROMPT_SPAN, PROMPT_SPAN, MAMBA_HEAD_COUNT) * block_scale[:, :, None]).reshape(PACKED_LENGTH, MAMBA_HEAD_COUNT)
    flurry_spans = jax.random.randint(flurry_seed_draw, (PACKED_LENGTH, 1), 0, PROMPT_SPAN) < 2
    return jnp.where(flurry_spans, 100.0, rescaled_amounts).astype(jnp.float32)


def draw_head_decay_rate(master_seed_draw, part):
    slow_key = jax.random.fold_in(master_seed_draw, 31)
    lowest = math.log(0.25 / MAXLEN)
    highest = math.log(0.05)
    return jnp.exp(jax.random.uniform(slow_key, (MAMBA_HEAD_COUNT,), jnp.float32, lowest, highest)).astype(jnp.float32)


def steps_of(rng, dims, cuts, low, largest):
    factor_of, own = 1.0, jax.random.fold_in(rng, 6)
    for axis_at, blocks in cuts:
        heights = jnp.exp(jax.random.uniform(jax.random.fold_in(own, axis_at), (blocks,), jnp.float32, low / len(cuts), largest / len(cuts)))
        factor_of = factor_of * jnp.repeat(heights, dims[axis_at] // blocks).reshape([-1 if axis == axis_at else 1 for axis in range(len(dims))])
    return factor_of


def length_profile(amount, total, limit, slope):
    weights = [(1 << 20) // math.isqrt(grade ** slope) + 1 for grade in range(2, amount + 1)]
    surplus, holding = total - limit - (amount - 1), [1] * (amount - 1)
    while surplus > 0:
        movable = [i for i in range(amount - 1) if holding[i] < limit]
        pool, budget = sum([weights[i] for i in movable]), surplus
        for i in movable:
            addition = min(limit - holding[i], max(1, budget * weights[i] // pool), surplus)
            holding[i] = holding[i] + addition
            surplus = surplus - addition
    return np.array([limit] + holding)


def ragged_sizes(key, number_of, total, most, lean):
    if number_of == 2:
        one = jax.random.randint(key, (), max(1, total - most), min(most, total - 1) + 1)
        return jnp.stack([one, total - one])
    tallies = jnp.asarray(length_profile(number_of, total, most, lean), jnp.int32)
    couples = (number_of - 1) // 2
    source_of, receiver = tallies[1:1 + 2 * couples:2], tallies[2:2 + 2 * couples:2]
    margin = jnp.minimum(source_of - 1, most - receiver)
    moved = jax.random.randint(jax.random.fold_in(key, 1), (couples,), 0, 1 << 20) % (margin + 1)
    tallies = tallies.at[1:1 + 2 * couples:2].set(source_of - moved).at[2:2 + 2 * couples:2].set(receiver + moved)
    return tallies[jax.random.permutation(jax.random.fold_in(key, 2), number_of)]


def centred(own_key, shape, scale, most, split=(), kind=jnp.bfloat16):
    entries = jax.random.normal(own_key, shape, jnp.float32) * scale
    if len(split) > 0:
        entries = steps_of(own_key, shape, split, -0.22, 0.18) * entries
    return jnp.clip(entries, min=-most, max=most).astype(kind)


def setup_inputs(seed: int = 0) -> dict:
    streams_of = jax.random.split(jax.random.key(seed), 22)
    hidden = centred(streams_of[0], (PACKED_LENGTH, MODEL_WIDTH), 1.0, 6.0, ((0, 16), (1, 8)))
    query_heads = draw_query_heads(jax.random.fold_in(streams_of[21], 71), 0)
    key_heads = draw_key_heads(jax.random.fold_in(streams_of[21], 71), 0)
    value_heads = centred(streams_of[3], (PACKED_LENGTH, HEADS_A * HD), 1.0, 6.0, ((0, 16), (1, 8)))
    segment_ids = jnp.searchsorted(jnp.cumsum(ragged_sizes(streams_of[4], NSEG, PACKED_LENGTH, MAXLEN, 3)), jnp.arange(PACKED_LENGTH), side="right").astype(jnp.int32)
    page_table = jax.vmap(lambda own: jax.random.permutation(own, PAGES_DEV))(jax.random.split(streams_of[5], N_REQ)).reshape((N_REQ, PAGES_DEV)).astype(jnp.int32)
    mamba_conv_input = centred(streams_of[6], (PACKED_LENGTH, MAMBA_HEAD_COUNT * MAMBA_HEAD_SIZE), 1.0, 6.0, ((0, 16), (1, 8)))
    mamba_output_gate = centred(streams_of[7], (PACKED_LENGTH, MAMBA_HEAD_COUNT * MAMBA_HEAD_SIZE), 1.0, 6.0, ((0, 16), (1, 8)))
    state_input_projection = centred(streams_of[8], (PACKED_LENGTH, STATE_GROUPS * STATE_SIZE), 1.0, 6.0, ((0, 16),))
    state_output_projection = centred(streams_of[9], (PACKED_LENGTH, STATE_GROUPS * STATE_SIZE), 1.0, 6.0, ((0, 16),))
    discrete_step_size = draw_discrete_step_size(jax.random.fold_in(streams_of[21], 71), 0)
    head_decay_rate = draw_head_decay_rate(jax.random.fold_in(streams_of[21], 71), 0)
    skip_gain = jnp.clip(0.5 + 1.5 * jax.random.uniform(streams_of[12], (MAMBA_HEAD_COUNT,), jnp.float32) ** steps_of(streams_of[12], (MAMBA_HEAD_COUNT,), ((0, 8),), -0.2, 0.2), 0.5, 2.0)
    mamba_gated_norm_gain = jnp.clip(1.0 + 0.18 * jax.random.normal(streams_of[13], (MAMBA_HEAD_COUNT * MAMBA_HEAD_SIZE,), jnp.float32), 0.1, 1.9)
    attn_proj = centred(streams_of[14], (HEADS_A * HD, MODEL_WIDTH), (HEADS_A * HD) ** -0.5, 0.09375, ((0, 8),))
    mamba_output_projection = centred(streams_of[15], (MAMBA_HEAD_COUNT * MAMBA_HEAD_SIZE, MODEL_WIDTH), (MAMBA_HEAD_COUNT * MAMBA_HEAD_SIZE) ** -0.5, 0.0625, ((0, 8),))
    mlp_norm_gain = jnp.clip(1.0 + 0.18 * jax.random.normal(streams_of[16], (MODEL_WIDTH,), jnp.float32), 0.1, 1.9)
    gate_proj = centred(streams_of[17], (MODEL_WIDTH, FF), MODEL_WIDTH ** -0.5, 0.09375, ((0, 16), (1, 8)))
    up_proj = centred(streams_of[18], (MODEL_WIDTH, FF), MODEL_WIDTH ** -0.5, 0.09375, ((0, 16), (1, 8)))
    down_proj = centred(streams_of[19], (FF, MODEL_WIDTH), FF ** -0.5, 0.0625, ((0, 8), (1, 16)))
    next_norm_gain = jnp.clip(1.0 + 0.18 * jax.random.normal(streams_of[20], (MODEL_WIDTH,), jnp.float32), 0.1, 1.9)
    return {"hidden": hidden, "query_heads": query_heads, "key_heads": key_heads, "value_heads": value_heads, "segment_ids": segment_ids, "page_table": page_table, "mamba_conv_input": mamba_conv_input, "mamba_output_gate": mamba_output_gate, "state_input_projection": state_input_projection, "state_output_projection": state_output_projection, "discrete_step_size": discrete_step_size, "head_decay_rate": head_decay_rate, "skip_gain": skip_gain, "mamba_gated_norm_gain": mamba_gated_norm_gain, "attn_proj": attn_proj, "mamba_output_projection": mamba_output_projection, "mlp_norm_gain": mlp_norm_gain, "gate_proj": gate_proj, "up_proj": up_proj, "down_proj": down_proj, "next_norm_gain": next_norm_gain}


EPSILON = 1e-05
exact_mode = lax.Precision.HIGHEST

def attend_rows(query_rows, segment_rows, pos_rows, key_block, value_block, key_segs, key_pos, head_count):
    row_total = query_rows.shape[0]
    key_total = key_block.shape[0]
    query_float = query_rows.astype(jnp.float32).reshape(row_total, head_count, HD)
    key_float = key_block.astype(jnp.float32).reshape(key_total, head_count, HD)
    value_float = value_block.astype(jnp.float32).reshape(key_total, head_count, HD)
    scores = jnp.einsum('qhd,khd->hqk', query_float, key_float) * (1.0 / math.sqrt(HD))
    allowed = (segment_rows[:, None] == key_segs[None, :]) & (key_pos[None, :] <= pos_rows[:, None])
    scores = jnp.where(allowed[None, :, :], scores, -jnp.inf)
    top_score = lax.optimization_barrier(jnp.max(scores, axis=2, keepdims=True))
    raised = jnp.exp(scores - top_score)
    weights = (raised / lax.optimization_barrier(jnp.sum(raised, axis=2, keepdims=True))).astype(jnp.bfloat16)
    summed = jnp.einsum('hqk,khd->qhd', weights.astype(jnp.float32), value_float)
    return summed.astype(jnp.bfloat16).reshape(row_total, head_count * HD)

def block_contributions(input_token_rows, input_proj_rows, output_proj_rows, step_size_rows, head_decay_rate, segment_rows, segment_prior_state, group_index, head_width):
    row_count = input_token_rows.shape[0]
    head_count = step_size_rows.shape[1]
    input_float = input_token_rows.astype(jnp.float32).reshape(row_count, head_count, head_width)
    b_float = input_proj_rows.astype(jnp.float32)
    c_float = output_proj_rows.astype(jnp.float32)
    running = jnp.cumsum(-step_size_rows * head_decay_rate[None, :], axis=0)
    positions = jnp.arange(row_count, dtype=jnp.int32)
    live = (segment_rows[:, None] == segment_rows[None, :]) & (positions[:, None] >= positions[None, :])
    spread = running.T[:, :, None] - running.T[:, None, :]
    mixing = jnp.exp(jnp.where(live[None, :, :], spread, -1e+30))
    inner = jnp.einsum('tgn,ugn->gtu', c_float, b_float, precision=exact_mode)
    driven = input_float * step_size_rows[:, :, None]
    local_output = jnp.einsum('htu,uhp->thp', mixing * inner[group_index], driven, precision=exact_mode)
    b_per_head = b_float[:, group_index, :]
    output_proj_per_head = c_float[:, group_index, :]
    tail_rows = segment_rows == segment_rows[row_count - 1]
    tail_gain = jnp.where(tail_rows[:, None], jnp.exp(running[row_count - 1][None, :] - running), 0.0)
    state_local_part = jnp.einsum('uh,uhp,uhn->hpn', tail_gain, driven, b_per_head, precision=exact_mode)
    decay_cumulative = jnp.where(segment_rows[row_count - 1] == segment_prior_state, jnp.exp(running[row_count - 1]), 0.0)
    entry_weighting = jnp.where((segment_rows == segment_prior_state)[:, None], jnp.exp(running), 0.0)
    return (local_output, decay_cumulative, state_local_part, entry_weighting, input_float, output_proj_per_head)

def finish(local_output, entry_weighting, input_float, output_proj_per_head, carry_in, skip_gain):
    carried = jnp.einsum('hpn,thn->thp', carry_in, output_proj_per_head, precision=exact_mode)
    result = local_output + entry_weighting[:, :, None] * carried + skip_gain[None, :, None] * input_float
    return result.reshape(result.shape[0], result.shape[1] * result.shape[2])

def reference(hidden, query_heads, key_heads, value_heads, segment_ids, page_table, mamba_conv_input, mamba_output_gate, state_input_projection, state_output_projection, discrete_step_size, head_decay_rate, skip_gain, mamba_gated_norm_gain, attn_proj, mamba_output_projection, mlp_norm_gain, gate_proj, up_proj, down_proj, next_norm_gain):
    lead_rows = REACH * PROMPT_SPAN
    feature_count = HEADS_A * HD
    key_padded = jnp.concatenate([jnp.zeros((lead_rows, feature_count), key_heads.dtype), key_heads], axis=0)
    value_padded = jnp.concatenate([jnp.zeros((lead_rows, feature_count), value_heads.dtype), value_heads], axis=0)
    seg_padded = jnp.concatenate([jnp.full((lead_rows,), -2, jnp.int32), segment_ids.astype(jnp.int32)])
    pos_padded = jnp.arange(PACKED_LENGTH + lead_rows, dtype=jnp.int32) - lead_rows

    def one_group(group_number):
        first_row = (group_number * PROMPT_SPAN).astype(jnp.int32)
        query_rows = lax.dynamic_slice_in_dim(query_heads, first_row, PROMPT_SPAN, 0)
        segment_rows = lax.dynamic_slice_in_dim(segment_ids, first_row, PROMPT_SPAN, 0)
        pos_rows = first_row + jnp.arange(PROMPT_SPAN, dtype=jnp.int32)
        key_block = lax.dynamic_slice_in_dim(key_padded, first_row, lead_rows + PROMPT_SPAN, 0)
        value_block = lax.dynamic_slice_in_dim(value_padded, first_row, lead_rows + PROMPT_SPAN, 0)
        key_segs = lax.dynamic_slice_in_dim(seg_padded, first_row, lead_rows + PROMPT_SPAN, 0)
        key_pos = lax.dynamic_slice_in_dim(pos_padded, first_row, lead_rows + PROMPT_SPAN, 0)
        return attend_rows(query_rows, segment_rows, pos_rows, key_block, value_block, key_segs, key_pos, HEADS_A)
    attended = lax.map(one_group, jnp.arange(N_REQ, dtype=jnp.int32)).reshape(PACKED_LENGTH, feature_count)
    page_total = N_REQ * PAGES_DEV

    def to_pages(source):
        return source.reshape(page_total, PAGE, HEADS_A, HD).transpose(2, 0, 1, 3).reshape(HEADS_A, page_total, PAGE * HD)
    target = (page_table.astype(jnp.int32) + PAGES_DEV * jnp.arange(N_REQ, dtype=jnp.int32)[:, None]).reshape(page_total)
    stacked = jnp.stack([to_pages(key_heads), to_pages(value_heads)])
    kv_cache = jnp.zeros_like(stacked).at[:, :, target].set(stacked)
    group_values = MAMBA_HEAD_COUNT // STATE_GROUPS
    head_group_index = (jnp.arange(MAMBA_HEAD_COUNT, dtype=jnp.int32) % STATE_GROUPS).astype(jnp.int32)
    segment_group_list = segment_ids.astype(jnp.int32).reshape(N_REQ, PROMPT_SPAN)
    segment_prior_state = jnp.concatenate([jnp.full((1,), -1, jnp.int32), segment_group_list[:-1, PROMPT_SPAN - 1]])
    sliced_values = (mamba_conv_input.reshape(N_REQ, PROMPT_SPAN, MAMBA_HEAD_COUNT * MAMBA_HEAD_SIZE), state_input_projection.reshape(N_REQ, PROMPT_SPAN, STATE_GROUPS, STATE_SIZE), state_output_projection.reshape(N_REQ, PROMPT_SPAN, STATE_GROUPS, STATE_SIZE), discrete_step_size.reshape(N_REQ, PROMPT_SPAN, MAMBA_HEAD_COUNT), segment_group_list, segment_prior_state)

    def advance_step(carried, pieces):
        input_token_rows, input_proj_rows, output_proj_rows, step_size_rows, segment_rows, prior_state = pieces
        local_output, decay_cumulative, state_local_part, entry_weighting, input_float, output_proj_per_head = block_contributions(input_token_rows, input_proj_rows, output_proj_rows, step_size_rows, head_decay_rate, segment_rows, prior_state, head_group_index, MAMBA_HEAD_SIZE)
        result = finish(local_output, entry_weighting, input_float, output_proj_per_head, carried, skip_gain)
        return (decay_cumulative[:, None, None] * carried + state_local_part, result)
    ignored_value, output_rows = lax.scan(advance_step, jnp.zeros((MAMBA_HEAD_COUNT, MAMBA_HEAD_SIZE, STATE_SIZE), jnp.float32), sliced_values)
    mamba_output = output_rows.reshape(PACKED_LENGTH, MAMBA_HEAD_COUNT * MAMBA_HEAD_SIZE)
    gated_output = mamba_output * jax.nn.silu(mamba_output_gate.astype(jnp.float32))
    grouped_values = gated_output.reshape(PACKED_LENGTH, MAMBA_HEAD_COUNT // STATE_GROUPS, STATE_GROUPS, MAMBA_HEAD_SIZE)
    group_mean = lax.optimization_barrier(jnp.sum(grouped_values * grouped_values, axis=(1, 3))) / (group_values * MAMBA_HEAD_SIZE)
    inverse_root_mean = lax.rsqrt(group_mean + EPSILON)
    mamba_normalized_rows = ((grouped_values * inverse_root_mean[:, None, :, None]).reshape(PACKED_LENGTH, MAMBA_HEAD_COUNT * MAMBA_HEAD_SIZE) * mamba_gated_norm_gain[None, :]).astype(jnp.bfloat16)
    mixed_rows = hidden.astype(jnp.float32) + jnp.dot(attended, attn_proj, preferred_element_type=jnp.float32) + jnp.dot(mamba_normalized_rows, mamba_output_projection, preferred_element_type=jnp.float32)
    normed = (mixed_rows * lax.rsqrt(lax.optimization_barrier(jnp.mean(mixed_rows * mixed_rows, axis=1, keepdims=True)) + EPSILON) * mlp_norm_gain[None, :]).astype(jnp.bfloat16)
    gate_act = jnp.dot(normed, gate_proj, preferred_element_type=jnp.float32)
    up_act = jnp.dot(normed, up_proj, preferred_element_type=jnp.float32)
    latent_activation = (jax.nn.silu(gate_act) * up_act).astype(jnp.bfloat16)
    new_hidden = (mixed_rows + jnp.dot(latent_activation, down_proj, preferred_element_type=jnp.float32)).astype(jnp.bfloat16)
    widened = new_hidden.astype(jnp.float32)
    next_normed = (widened * lax.rsqrt(lax.optimization_barrier(jnp.mean(widened * widened, axis=1, keepdims=True)) + EPSILON) * next_norm_gain[None, :]).astype(jnp.bfloat16)
    return (new_hidden, next_normed, kv_cache)
```

```python
import math

import jax
import jax.numpy as jnp
from jax import lax
from jax.experimental import pallas as pl
from jax.experimental.pallas import tpu as pltpu
from jax.sharding import Mesh
from jax.sharding import PartitionSpec as P

HD = 224
PAGE = 16
EPS = 1e-05
LOG2E = math.log2(math.e)
T = 512
F32 = jnp.float32
BF16 = jnp.bfloat16
REQ = ("z", "y")
MLP = ("x", "c")
VMEM = pltpu.CompilerParams(vmem_limit_bytes=56 << 20)


def dot(a, b, ca=1, cb=0):
    return lax.dot_general(a, b, (((ca,), (cb,)), ((), ())), preferred_element_type=F32)


def lanes_of(shape):
    return lax.broadcasted_iota(jnp.int32, shape, 1)


def halves(pair, i, rows, base=0):
    low = jnp.broadcast_to(pair[:, base + 2 * i : base + 2 * i + 1], (rows, 128))
    high = jnp.broadcast_to(pair[:, base + 2 * i + 1 : base + 2 * i + 2], (rows, 128))
    return jnp.where(lanes_of((rows, 128)) < 64, low, high)


def state_kernel(dt_ref, rate_ref, seg_ref, x_ref, b_ref, state_ref, row_ref, col_ref, tmp_ref):
    heads = dt_ref.shape[0]
    tiles = x_ref.shape[1] // 128
    tmp_ref[...] = jnp.zeros_like(tmp_ref)
    tmp_ref[0:heads, :] = dt_ref[...] * (rate_ref[...] * -LOG2E)
    tmp_ref[16:32, :] = jnp.ones((16, T), F32)
    tmp_ref[16 : 16 + heads, :] = dt_ref[...]
    run = tmp_ref[0:16, :]
    lane = lanes_of((16, T))
    shift = 1
    while shift < T:
        run = run + jnp.where(lane >= shift, pltpu.roll(run, shift, 1), 0.0)
        shift *= 2
    row = run - jnp.log2(tmp_ref[16:32, :])
    row_ref[...] = row
    last = jnp.sum(jnp.where(lane == T - 1, run, 0.0), axis=1, keepdims=True)
    seg = seg_ref[...]
    tail = jnp.where(seg == jnp.max(seg), 1.0, 0.0)
    tmp_ref[0:16, :] = run
    tmp_ref[16:32, :] = jnp.exp2(last - row) * tail
    col = tmp_ref[...].T
    col_ref[...] = col
    b_rows = b_ref[...].astype(F32).T.astype(BF16)
    for i in range(tiles):
        cut = slice(128 * i, 128 * i + 128)
        weighted = (x_ref[:, cut].astype(F32) * halves(col, i, T, 16)).astype(BF16)
        both = dot(b_rows, weighted)
        kept = jnp.where(lanes_of((64, 128)) < 64, both[0:64], both[64:128])
        state_ref[0:64, cut] = kept.astype(BF16)
        gone = jnp.exp2(halves(col[T - 8 : T], i, 8))[7:8]
        state_ref[64:80, cut] = jnp.broadcast_to(gone, (16, 128)).astype(BF16)


def leaving_state(dt_rows, rate, seg_row, x, b):
    width = x.shape[1]
    return pl.pallas_call(
        state_kernel,
        out_shape=(
            jax.ShapeDtypeStruct((80, width), BF16),
            jax.ShapeDtypeStruct((16, T), F32),
            jax.ShapeDtypeStruct((T, 128), F32),
        ),
        scratch_shapes=[pltpu.VMEM((128, T), F32)],
        compiler_params=VMEM,
        name="leaving_state",
    )(dt_rows, rate, seg_row, x, b)


HALF = T // 2


def mamba_kernel(
    x_ref, z_ref, b_ref, c_ref, row_ref, col_ref, segr_ref, segc_ref, near_ref, far_ref,
    ids1_ref, ids2_ref, skip_ref, out_ref, sq_ref, inner_ref,
):
    tiles = x_ref.shape[1] // 128
    b = b_ref[...]
    c = c_ref[...]
    live = (segc_ref[...] == segr_ref[...]) & (
        lax.broadcasted_iota(jnp.int32, (T, T), 0) >= lanes_of((T, T))
    )
    group = lanes_of((T, 128)) < 64
    for g in range(2):
        own = jnp.where(group == (g == 0), c, jnp.zeros_like(c))
        inner_ref[g] = jnp.where(live, dot(own, b, 1, 1), 0.0)
    last1 = jnp.max(ids1_ref[...].astype(F32))
    last2 = jnp.max(ids2_ref[...].astype(F32))
    passes = jnp.where(last1 == last2, 1.0, 0.0)
    enters = segc_ref[...].astype(F32) + 1.0 == last1
    col = col_ref[...]
    entry = jnp.where(enters, jnp.exp2(col), 0.0)
    low = lanes_of((HALF, 128)) < 64
    totals = [jnp.zeros((HALF, 128), F32) for _ in range(2)]
    for i in range(tiles):
        cut = slice(128 * i, 128 * i + 128)
        carry = (
            near_ref[0:64, cut].astype(F32)
            + near_ref[64:65, cut].astype(F32) * passes * far_ref[0:64, cut].astype(F32)
        ).astype(BF16)
        first = lanes_of((64, 128)) < 64
        nothing = jnp.zeros_like(carry)
        spread_state = jnp.concatenate(
            [jnp.where(first, carry, nothing), jnp.where(first, nothing, carry)], axis=0
        )
        for k in range(2):
            rows = slice(HALF * k, HALF * k + HALF)
            upto = HALF * (k + 1)
            parts = []
            for g in range(2):
                j = 2 * i + g
                power = jnp.minimum(col[rows, j : j + 1] - row_ref[j : j + 1, 0:upto], 126.0)
                mixing = (jnp.exp2(power) * inner_ref[g, rows, 0:upto]).astype(BF16)
                parts.append(dot(mixing, x_ref[0:upto, cut]))
            y = jnp.where(low, parts[0], parts[1])
            y = y + halves(entry[rows], i, HALF) * dot(c[rows], spread_state)
            y = y + skip_ref[:, cut] * x_ref[rows, cut].astype(F32)
            z = z_ref[rows, cut].astype(F32)
            gated = y * (z / (1.0 + jnp.exp(-z)))
            out_ref[rows, cut] = gated
            totals[k] = totals[k] + gated * gated
    for k in range(2):
        turned = totals[k].T
        even = jnp.sum(turned[0:64], axis=0, keepdims=True)
        odd = jnp.sum(turned[64:128], axis=0, keepdims=True)
        sq_ref[:, HALF * k : HALF * k + HALF] = jnp.concatenate([even, odd], axis=0)


def mamba_outputs(x, z, b, c, row, col, seg_row, seg_col, near, far, kv1, kv2, skip):
    width = x.shape[1]
    whole = lambda a: pl.BlockSpec(a.shape, lambda s: (0,) * a.ndim)
    ids = pl.BlockSpec((16, T), lambda s: (kv1.shape[0] // 16 - 1, 0))
    args = [x, z, b, c, row, col, seg_row, seg_col, near, far]
    return pl.pallas_call(
        mamba_kernel,
        grid=(1,),
        out_shape=(jax.ShapeDtypeStruct((T, width), F32), jax.ShapeDtypeStruct((2, T), F32)),
        in_specs=[*map(whole, args), ids, ids, whole(skip)],
        out_specs=(
            pl.BlockSpec((T, width), lambda s: (0, 0)), pl.BlockSpec((2, T), lambda s: (0, 0))
        ),
        scratch_shapes=[pltpu.VMEM((2, T, T), F32)],
        compiler_params=VMEM,
        name="mamba_outputs",
    )(*args, kv1, kv2, skip)


def attention_kernel(
    q_ref, k0_ref, v0_ref, k1_ref, v1_ref, k2_ref, v2_ref, ids1_ref, ids2_ref, segr_ref, segc_ref, out_ref
):
    q = q_ref[...]
    seg = segc_ref[...]
    mine = seg.astype(F32) + 1.0
    scale = LOG2E / math.sqrt(HD)
    causal = (seg == segr_ref[...]) & (
        lax.broadcasted_iota(jnp.int32, (T, T), 0) >= lanes_of((T, T))
    )
    parts = []
    for k_ref, allowed in (
        (k0_ref, causal),
        (k1_ref, mine == ids1_ref[0:1, :].astype(F32)),
        (k2_ref, mine == ids2_ref[0:1, :].astype(F32)),
    ):
        parts.append(jnp.where(allowed, dot(q, k_ref[...], 0, 0) * scale, -jnp.inf))
    top = jnp.max(jnp.maximum(jnp.maximum(parts[0], parts[1]), parts[2]), axis=1, keepdims=True)
    raised = [jnp.exp2(part - top) for part in parts]
    total = jnp.sum(raised[0] + raised[1] + raised[2], axis=1, keepdims=True)
    share = 1.0 / total
    weights = [(part * share).astype(BF16) for part in raised]
    out = dot(v0_ref[...], weights[0], 1, 1)
    out = out + dot(v1_ref[...], weights[1], 1, 1)
    out = out + dot(v2_ref[...], weights[2], 1, 1)
    out_ref[...] = out.astype(BF16)


def attend(q, k, v, kv1, kv2, seg_row, seg_col):
    width = q.shape[0]
    heads = width // HD
    head = pl.BlockSpec((HD, T), lambda h: (h, 0))
    value = pl.BlockSpec((HD, T), lambda h: (heads + h, 0))
    ids = pl.BlockSpec((16, T), lambda h: (kv1.shape[0] // 16 - 1, 0))
    return pl.pallas_call(
        attention_kernel,
        grid=(heads,),
        out_shape=jax.ShapeDtypeStruct((width, T), BF16),
        in_specs=[
            head, head, head, head, value, head, value, ids, ids,
            pl.BlockSpec((1, T), lambda h: (0, 0)), pl.BlockSpec((T, 1), lambda h: (0, 0)),
        ],
        out_specs=head,
        compiler_params=VMEM,
        name="attend",
    )(q, k, v, kv1, kv1, kv2, kv2, kv1, kv2, seg_row, seg_col)


NT = 256


def project_kernel(att_ref, gated_ref, sq_ref, gain_ref, wa_ref, wm_ref, out_ref, att_s, mam_s):
    @pl.when(pl.program_id(0) == 0)
    def _():
        att_s[...] = att_ref[...].astype(F32).T.astype(BF16)
        tiles = gated_ref.shape[1] // 128
        inverse = lax.rsqrt(sq_ref[...] / (tiles * 64 * 8) + EPS)
        spread = jnp.concatenate(
            [jnp.broadcast_to(inverse[0:1], (64, T)), jnp.broadcast_to(inverse[1:2], (64, T))], axis=0
        ).T
        for i in range(tiles):
            cut = slice(128 * i, 128 * i + 128)
            mam_s[:, cut] = (gated_ref[:, cut] * spread * gain_ref[:, cut]).astype(BF16)

    out = dot(att_s[...], wa_ref[...]) + dot(mam_s[...], wm_ref[...])
    out_ref[...] = out.T.astype(BF16)


def project(att, gated, squares, gain, wa, wm):
    total = wa.shape[1]
    same = lambda a: pl.BlockSpec(a.shape, lambda n: (0,) * a.ndim)
    return pl.pallas_call(
        project_kernel,
        grid=(total // NT,),
        out_shape=jax.ShapeDtypeStruct((total, T), BF16),
        in_specs=[
            same(att), same(gated), same(squares), same(gain),
            pl.BlockSpec((wa.shape[0], NT), lambda n: (0, n)),
            pl.BlockSpec((wm.shape[0], NT), lambda n: (0, n)),
        ],
        out_specs=pl.BlockSpec((NT, T), lambda n: (n, 0)),
        scratch_shapes=[pltpu.VMEM((T, att.shape[0]), BF16), pltpu.VMEM(gated.shape, BF16)],
        compiler_params=VMEM,
        name="project",
    )(att, gated, squares, gain, wa, wm)


def mlp_kernel(x_ref, unscale_ref, gu_ref, down_ref, out_ref, rows_s, inv_s, act_s):
    step = pl.program_id(0)
    first = act_s.shape[1] // 128

    @pl.when(step == 0)
    def _():
        width = x_ref.shape[0]
        total = jnp.zeros((T, 128), F32)
        for i in range(width // 128):
            cut = slice(128 * i, 128 * i + 128)
            turned = x_ref[cut, :].astype(F32).T
            rows_s[:, cut] = turned.astype(BF16)
            plain = turned * unscale_ref[:, cut]
            total = total + plain * plain
        inv_s[...] = jnp.broadcast_to(
            lax.rsqrt(jnp.sum(total, axis=1, keepdims=True) / width + EPS), (T, 128)
        )

    @pl.when(step < first)
    def _():
        width = x_ref.shape[0]
        gate_w = gu_ref[:, 0].reshape(width, 128)
        up_w = gu_ref[:, 1].reshape(width, 128)
        both = dot(rows_s[...], jnp.concatenate([gate_w, up_w], axis=1))
        gate = both[:, 0:128] * inv_s[...]
        up = both[:, 128:256] * inv_s[...]
        act_s[:, pl.ds(pl.multiple_of(step * 128, 128), 128)] = (
            gate / (1.0 + jnp.exp(-gate)) * up
        ).astype(BF16)

    @pl.when(step >= first)
    def _():
        w = down_ref[:, 0].reshape(out_ref.shape[0], act_s.shape[1])
        out_ref[...] = dot(w, act_s[...], 1, 1).astype(BF16)


def mlp(x, unscale, weights):
    width = x.shape[0]
    parts, _, rows, hidden = weights.shape
    first = hidden // 128
    blocks = 4
    per = parts // blocks
    return pl.pallas_call(
        mlp_kernel,
        grid=(first + blocks,),
        out_shape=jax.ShapeDtypeStruct((width, T), BF16),
        in_specs=[
            pl.BlockSpec((width, T), lambda s: (0, 0)),
            pl.BlockSpec((1, width), lambda s: (0, 0)),
            pl.BlockSpec((parts, 2, rows, 128), lambda s: (0, 0, 0, jnp.minimum(s, first - 1))),
            pl.BlockSpec((per, 1, rows, hidden), lambda s: (jnp.maximum(s - first, 0), 2, 0, 0)),
        ],
        out_specs=pl.BlockSpec((per * rows, T), lambda s: (jnp.maximum(s - first, 0), 0)),
        scratch_shapes=[
            pltpu.VMEM((T, width), BF16), pltpu.VMEM((T, 128), F32), pltpu.VMEM((T, hidden), BF16)
        ],
        compiler_params=VMEM,
        name="mlp",
    )(x, unscale, weights, weights)


def behind(value, steps):
    count = lax.axis_size(REQ)
    return lax.ppermute(value, REQ, [(i, i + steps) for i in range(count - steps)])


def along(value, steps):
    count = lax.axis_size("x")
    return lax.ppermute(value, "x", [(i, (i + steps) % count) for i in range(count)])


def swap(value):
    return lax.ppermute(value, "c", [(0, 1), (1, 0)])


def scatter_sum(partial):
    count = lax.axis_size("x")
    x, c = lax.axis_index("x"), lax.axis_index("c")
    rows = partial.shape[0] // (2 * count)
    blocks = partial.reshape(count, 2, rows, partial.shape[1])
    mine = lax.dynamic_index_in_dim(blocks, c, 1, keepdims=False)
    other = lax.dynamic_index_in_dim(blocks, 1 - c, 1, keepdims=False)
    paired = mine.astype(F32) + swap(other).astype(F32)
    total = lax.dynamic_index_in_dim(paired, x, 0, keepdims=False)
    narrow = paired.astype(BF16)
    for d in range(1, count):
        out = lax.dynamic_index_in_dim(narrow, (x + d) % count, 0, keepdims=False)
        total = total + along(out, d).astype(F32)
    return total


def gather_rows(share):
    count = lax.axis_size("x")
    x, c = lax.axis_index("x"), lax.axis_index("c")
    rows, cols = share.shape
    got = jnp.zeros((count, rows, cols), share.dtype)
    got = lax.dynamic_update_index_in_dim(got, share, x, 0)
    for d in range(1, count):
        got = lax.dynamic_update_index_in_dim(got, along(share, d), (x - d) % count, 0)
    other = swap(got)
    full = jnp.zeros((count, 2, rows, cols), share.dtype)
    full = lax.dynamic_update_index_in_dim(full, got, c, 1)
    full = lax.dynamic_update_index_in_dim(full, other, 1 - c, 1)
    return full.reshape(2 * count * rows, cols)


def body(
    hidden, query_heads, key_heads, value_heads, segment_ids, page_table, mamba_conv_input,
    mamba_output_gate, state_input_projection, state_output_projection, discrete_step_size,
    head_decay_rate, skip_gain, mamba_gated_norm_gain, attn_proj, mamba_output_projection,
    mlp_norm_gain, gate_proj, up_proj, down_proj, next_norm_gain,
):
    row_count = query_heads.shape[0]
    head_count = query_heads.shape[1] // HD
    width = hidden.shape[1]
    total_width = mlp_norm_gain.shape[0]
    owner = lax.axis_index("x") * lax.axis_size("c") + lax.axis_index("c")

    stacked_weights = jnp.stack([gate_proj, up_proj, down_proj.T])
    weights = lax.all_gather(stacked_weights, REQ, axis=0, tiled=False)

    q, k, v = query_heads.T, key_heads.T, value_heads.T
    ids = jnp.broadcast_to((segment_ids + 1).astype(BF16)[None, :], (16, row_count))
    payload = jnp.concatenate([k, v, ids], axis=0)
    kv1, kv2 = behind(payload, 1), behind(payload, 2)

    seg_row = segment_ids.reshape(1, row_count)
    seg_col = segment_ids.reshape(row_count, 1)
    state, row, col = leaving_state(
        discrete_step_size.T, head_decay_rate.reshape(-1, 1), seg_row, mamba_conv_input,
        state_input_projection,
    )
    near, far = behind(state, 1), behind(state, 2)
    skip = jnp.repeat(skip_gain, mamba_conv_input.shape[1] // skip_gain.shape[0]).reshape(1, -1)
    gated, squares = mamba_outputs(
        mamba_conv_input, mamba_output_gate, state_input_projection, state_output_projection,
        row, col, seg_row, seg_col, near, far, kv1, kv2, skip,
    )
    squares = lax.psum(squares, MLP)
    attended = attend(q, k, v, kv1, kv2, seg_row, seg_col)
    projected = project(
        attended, gated, squares, mamba_gated_norm_gain.reshape(1, -1), attn_proj,
        mamba_output_projection,
    )
    mixed = scatter_sum(projected) + hidden.T.astype(F32)
    own_gain = lax.dynamic_slice_in_dim(mlp_norm_gain, owner * width, width, 0)
    scaled = gather_rows((mixed * own_gain[:, None]).astype(BF16))
    partial = mlp(scaled, (1.0 / mlp_norm_gain).reshape(1, -1), weights)
    new_hidden = (mixed + scatter_sum(partial)).astype(BF16)
    widened = new_hidden.astype(F32)
    total_sq = lax.psum(jnp.sum(widened * widened, axis=0), MLP)
    next_normed = (
        widened * lax.rsqrt(total_sq / total_width + EPS)[None, :] * next_norm_gain[:, None]
    ).astype(BF16)

    page_count = page_table.shape[1]

    def to_pages(source):
        return (
            source.reshape(page_count, PAGE, head_count, HD)
            .transpose(2, 0, 1, 3)
            .reshape(head_count, page_count, PAGE * HD)
        )

    stacked = jnp.stack([to_pages(key_heads), to_pages(value_heads)])
    kv_cache = jnp.zeros_like(stacked).at[:, :, page_table[0]].set(stacked)
    return (new_hidden.T, next_normed.T, kv_cache)


def solution(mesh):
    split = Mesh(mesh.devices.reshape(4, 4, 4, 2), ("z", "y", "x", "c"))
    tokens = P(REQ, MLP)
    return jax.shard_map(
        body,
        mesh=split,
        in_specs=(
            tokens, tokens, tokens, tokens, P(REQ), P(REQ, None), tokens, tokens, P(REQ, None),
            P(REQ, None), tokens, P(MLP), P(MLP), P(MLP), P(MLP, None), P(MLP, None), P(), tokens,
            tokens, P(MLP, REQ), P(MLP),
        ),
        out_specs=(tokens, tokens, P(None, MLP, REQ, None)),
        check_vma=False,
    )
```

```python
import math

import jax
import jax.numpy as jnp
from jax import lax
from jax.experimental import pallas as pl
from jax.experimental.pallas import tpu as pltpu
from jax.sharding import Mesh
from jax.sharding import PartitionSpec as P

HD = 224
PAGE = 16
EPS = 1e-05
LOG2E = math.log2(math.e)
T = 512
F32 = jnp.float32
BF16 = jnp.bfloat16
REQ = ("z", "y")
MLP = ("x", "c")


def vmem(mib):
    return pltpu.CompilerParams(vmem_limit_bytes=mib << 20)


def in_hbm(value):
    return pltpu.with_memory_space_constraint(value, pltpu.HBM)


def dot(a, b, ca=1, cb=0):
    return lax.dot_general(a, b, (((ca,), (cb,)), ((), ())), preferred_element_type=F32)


def lanes_of(shape):
    return lax.broadcasted_iota(jnp.int32, shape, 1)


def halves(pair, i, rows, base=0):
    low = jnp.broadcast_to(pair[:, base + 2 * i : base + 2 * i + 1], (rows, 128))
    high = jnp.broadcast_to(pair[:, base + 2 * i + 1 : base + 2 * i + 2], (rows, 128))
    return jnp.where(lanes_of((rows, 128)) < 64, low, high)


def state_kernel(dt_ref, rate_ref, seg_ref, x_ref, b_ref, state_ref, row_ref, col_ref, tmp_ref):
    heads = dt_ref.shape[0]
    tiles = x_ref.shape[1] // 128
    tmp_ref[...] = jnp.zeros_like(tmp_ref)
    tmp_ref[0:heads, :] = dt_ref[...] * (rate_ref[...] * -LOG2E)
    tmp_ref[16:32, :] = jnp.ones((16, T), F32)
    tmp_ref[16 : 16 + heads, :] = dt_ref[...]
    run = tmp_ref[0:16, :]
    lane = lanes_of((16, T))
    shift = 1
    while shift < T:
        run = run + jnp.where(lane >= shift, pltpu.roll(run, shift, 1), 0.0)
        shift *= 2
    row = run - jnp.log2(tmp_ref[16:32, :])
    row_ref[...] = row
    last = jnp.sum(jnp.where(lane == T - 1, run, 0.0), axis=1, keepdims=True)
    seg = seg_ref[...]
    tail = jnp.where(seg == jnp.max(seg), 1.0, 0.0)
    tmp_ref[0:16, :] = run
    tmp_ref[16:32, :] = jnp.exp2(last - row) * tail
    col = tmp_ref[...].T
    col_ref[...] = col
    b_rows = b_ref[...].astype(F32).T.astype(BF16)
    for i in range(tiles):
        cut = slice(128 * i, 128 * i + 128)
        weighted = (x_ref[:, cut].astype(F32) * halves(col, i, T, 16)).astype(BF16)
        both = dot(b_rows, weighted)
        kept = jnp.where(lanes_of((64, 128)) < 64, both[0:64], both[64:128])
        state_ref[0:64, cut] = kept.astype(BF16)
        gone = jnp.exp2(halves(col[T - 8 : T], i, 8))[7:8]
        final = jnp.broadcast_to((jnp.max(seg) + 1).astype(F32), (8, 128))
        state_ref[64:80, cut] = jnp.concatenate(
            [jnp.broadcast_to(gone, (8, 128)), final], axis=0
        ).astype(BF16)


def leaving_state(dt_rows, rate, seg_row, x, b):
    width = x.shape[1]
    return pl.pallas_call(
        state_kernel,
        out_shape=(
            jax.ShapeDtypeStruct((80, width), BF16),
            jax.ShapeDtypeStruct((16, T), F32),
            jax.ShapeDtypeStruct((T, 128), F32),
        ),
        scratch_shapes=[pltpu.VMEM((128, T), F32)],
        compiler_params=vmem(12),
        name="leaving_state",
    )(dt_rows, rate, seg_row, x, b)


def through_kernel(state_ref, near_ref, out_ref):
    tail = state_ref[64:80, :].astype(F32)
    before = near_ref[64:80, :].astype(F32)
    passes = jnp.where(tail[8:9] == before[8:9], tail[0:1], 0.0)
    out_ref[0:64, :] = (
        state_ref[0:64, :].astype(F32) + passes * near_ref[0:64, :].astype(F32)
    ).astype(BF16)
    out_ref[64:80, :] = state_ref[64:80, :]


def pass_through(state, near):
    return pl.pallas_call(
        through_kernel,
        out_shape=jax.ShapeDtypeStruct(state.shape, BF16),
        compiler_params=vmem(4),
        name="pass_through",
    )(state, near)


HALF = T // 2


def local_kernel(x_ref, b_ref, c_ref, row_ref, col_ref, segr_ref, segc_ref, skip_ref, out_ref, inner_ref):
    tiles = x_ref.shape[1] // 128
    b = b_ref[...]
    c = c_ref[...]
    live = (segc_ref[...] == segr_ref[...]) & (
        lax.broadcasted_iota(jnp.int32, (T, T), 0) >= lanes_of((T, T))
    )
    group = lanes_of((T, 128)) < 64
    for g in range(2):
        own = jnp.where(group == (g == 0), c, jnp.zeros_like(c))
        inner_ref[g] = jnp.where(live, dot(own, b, 1, 1), 0.0)
    col = col_ref[...]
    lane = lanes_of((T, 128))
    low = lanes_of((HALF, 128)) < 64

    def tile(i, _):
        cut = pl.ds(pl.multiple_of(i * 128, 128), 128)
        decays = [
            jnp.sum(jnp.where(lane == 2 * i + g, col, 0.0), axis=1, keepdims=True) for g in range(2)
        ]
        rows_of = [row_ref[pl.ds(2 * i + g, 1), :] for g in range(2)]
        for k in range(2):
            rows = slice(HALF * k, HALF * k + HALF)
            upto = HALF * (k + 1)
            parts = []
            for g in range(2):
                power = jnp.minimum(decays[g][rows] - rows_of[g][:, 0:upto], 126.0)
                mixing = (jnp.exp2(power) * inner_ref[g, rows, 0:upto]).astype(BF16)
                parts.append(dot(mixing, x_ref[0:upto, cut]))
            y = jnp.where(low, parts[0], parts[1])
            out_ref[rows, cut] = y + skip_ref[:, cut] * x_ref[rows, cut].astype(F32)
        return 0

    lax.fori_loop(0, tiles, tile, 0)


def mamba_local(x, b, c, row, col, seg_row, seg_col, skip):
    return pl.pallas_call(
        local_kernel,
        out_shape=jax.ShapeDtypeStruct(x.shape, F32),
        scratch_shapes=[pltpu.VMEM((2, T, T), F32)],
        compiler_params=vmem(14),
        name="mamba_local",
    )(x, b, c, row, col, seg_row, seg_col, skip)


def finish_kernel(y_ref, z_ref, c_ref, col_ref, segc_ref, carry_ref, out_ref, sq_ref):
    tiles = y_ref.shape[1] // 128
    c = c_ref[...]
    last = jnp.max(carry_ref[64:80, 0:128].astype(F32)[8:16])
    enters = segc_ref[...].astype(F32) + 1.0 == last
    entry = jnp.where(enters, jnp.exp2(col_ref[...]), 0.0)
    first = lanes_of((64, 128)) < 64
    total = jnp.zeros((T, 128), F32)
    for i in range(tiles):
        cut = slice(128 * i, 128 * i + 128)
        carry = carry_ref[0:64, cut]
        nothing = jnp.zeros_like(carry)
        spread_state = jnp.concatenate(
            [jnp.where(first, carry, nothing), jnp.where(first, nothing, carry)], axis=0
        )
        y = y_ref[:, cut] + halves(entry, i, T) * dot(c, spread_state)
        z = z_ref[:, cut].astype(F32)
        gated = y * (z / (1.0 + jnp.exp(-z)))
        out_ref[:, cut] = gated
        total = total + gated * gated
    turned = total.T
    even = jnp.sum(turned[0:64], axis=0, keepdims=True)
    odd = jnp.sum(turned[64:128], axis=0, keepdims=True)
    sq_ref[...] = jnp.concatenate([even, odd], axis=0)


def mamba_finish(y, z, c, col, seg_col, carry):
    return pl.pallas_call(
        finish_kernel,
        out_shape=(jax.ShapeDtypeStruct(y.shape, F32), jax.ShapeDtypeStruct((2, T), F32)),
        compiler_params=vmem(14),
        name="mamba_finish",
    )(y, z, c, col, seg_col, carry)


def normalize_kernel(gated_ref, sq_ref, gain_ref, out_ref):
    tiles = gated_ref.shape[1] // 128
    inverse = lax.rsqrt(sq_ref[...] / (tiles * 64 * 8) + EPS)
    spread = jnp.concatenate(
        [jnp.broadcast_to(inverse[0:1], (64, T)), jnp.broadcast_to(inverse[1:2], (64, T))], axis=0
    )
    for i in range(tiles):
        cut = slice(128 * i, 128 * i + 128)
        out_ref[cut, :] = ((gated_ref[:, cut] * gain_ref[:, cut]).T * spread).astype(BF16)


def normalize(gated, squares, gain):
    return pl.pallas_call(
        normalize_kernel,
        out_shape=jax.ShapeDtypeStruct(gated.shape[::-1], BF16),
        compiler_params=vmem(10),
        name="normalize",
    )(gated, squares, gain)


NONE = -1e30


def softmax_of(parts, values):
    top = parts[0]
    for part in parts[1:]:
        top = jnp.maximum(top, part)
    top = jnp.maximum(jnp.max(top, axis=0, keepdims=True), NONE)
    raised = [jnp.exp2(part - top) for part in parts]
    total = sum(raised)
    total = jnp.sum(total, axis=0, keepdims=True)
    some = total > 0.0
    safe = jnp.where(some, total, 1.0)
    share = jnp.where(some, 1.0 / safe, 0.0)
    out = sum(dot(value, (part * share).astype(BF16)) for part, value in zip(raised, values))
    return out, jnp.where(some, top + jnp.log2(safe), NONE)


def own_kernel(q_ref, k_ref, v_ref, segr_ref, segc_ref, out_ref, lse_ref):
    scale = LOG2E / math.sqrt(HD)
    mask = (segc_ref[...] == segr_ref[...]) & (
        lax.broadcasted_iota(jnp.int32, (T, T), 0) <= lanes_of((T, T))
    )
    lse_ref[...] = jnp.zeros_like(lse_ref)
    for h in range(q_ref.shape[0] // HD):
        at = slice(HD * h, HD * h + HD)
        part = jnp.where(mask, dot(k_ref[at, :], q_ref[at, :], 0, 0) * scale, -jnp.inf)
        out_ref[at, :], lse_ref[h : h + 1, :] = softmax_of([part], [v_ref[at, :]])


def attend_own(q, k, v, seg_row, seg_col):
    return pl.pallas_call(
        own_kernel,
        out_shape=(jax.ShapeDtypeStruct(q.shape, F32), jax.ShapeDtypeStruct((8, T), F32)),
        compiler_params=vmem(12),
        name="attend_own",
    )(q, k, v, seg_row, seg_col)


def next_kernel(q_ref, k_ref, v_ref, kv_ref, segc_ref, out_ref):
    width = k_ref.shape[0]
    scale = LOG2E / math.sqrt(HD)
    wanted = q_ref[width : width + 16, :].astype(F32)[0:1]
    ids = kv_ref[2 * width : 2 * width + 16, :].astype(F32)[0:8]
    before = jnp.concatenate([ids] * 16, axis=0).T[:, 0:1]
    masks = (segc_ref[...].astype(F32) + 1.0 == wanted, before == wanted)
    rows = []
    for h in range(width // HD):
        at = slice(HD * h, HD * h + HD)
        theirs = slice(width + HD * h, width + HD * h + HD)
        keys, values = (k_ref[at, :], kv_ref[at, :]), (v_ref[at, :], kv_ref[theirs, :])
        parts = [
            jnp.where(mask, dot(key, q_ref[at, :], 0, 0) * scale, -jnp.inf)
            for mask, key in zip(masks, keys)
        ]
        out, lse = softmax_of(parts, values)
        out_ref[at, :] = out.astype(BF16)
        for _ in range(3):
            rows.append(lse.astype(BF16).astype(F32))
            lse = lse - rows[-1]
    rows.append(jnp.ones((16 - len(rows), T), F32))
    out_ref[width : width + 16, :] = jnp.concatenate(rows, axis=0).astype(BF16)


def attend_next(q, k, v, kv, seg_col):
    return pl.pallas_call(
        next_kernel,
        out_shape=jax.ShapeDtypeStruct(q.shape, BF16),
        compiler_params=vmem(14),
        name="attend_next",
    )(q, k, v, kv, seg_col)


def merge_kernel(out_ref, lse_ref, far_ref, rows_ref):
    width = out_ref.shape[0]
    stats = far_ref[width : width + 16, :].astype(F32)
    given = stats[15:16] > 0.0
    merged = []
    for h in range(width // HD):
        at = slice(HD * h, HD * h + HD)
        lse = stats[3 * h : 3 * h + 1] + stats[3 * h + 1 : 3 * h + 2] + stats[3 * h + 2 : 3 * h + 3]
        lse = jnp.where(given, lse, NONE)
        own = lse_ref[h : h + 1, :]
        top = jnp.maximum(lse, own)
        near, far = jnp.exp2(own - top), jnp.exp2(lse - top)
        total = near + far
        merged.append(
            out_ref[at, :] * (near / total) + far_ref[at, :].astype(F32) * (far / total)
        )
    rows_ref[...] = jnp.concatenate(merged, axis=0).astype(BF16)


def merge(out, lse, far):
    return pl.pallas_call(
        merge_kernel,
        out_shape=jax.ShapeDtypeStruct(out.shape, BF16),
        compiler_params=vmem(8),
        name="merge",
    )(out, lse, far)


def project_kernel(place_ref, att_ref, mam_ref, wa_ref, wm_ref, own_ref, other_ref):
    half = own_ref.shape[0]
    out = dot(wa_ref[...], att_ref[...], 0, 0) + dot(wm_ref[...], mam_ref[...], 0, 0)
    first = place_ref[1] == 0
    own_ref[...] = jnp.where(first, out[0:half], out[half:])
    other_ref[...] = jnp.where(first, out[half:], out[0:half]).astype(BF16)


def project(place, att, mam, wa, wm):
    rows = wa.shape[0]
    once = pl.Buffered(1)
    block = pl.BlockSpec((rows, T), lambda s, p: (0, 0), pipeline_mode=once)
    return pl.pallas_call(
        project_kernel,
        grid_spec=pltpu.PrefetchScalarGridSpec(
            num_scalar_prefetch=1,
            grid=(1,),
            in_specs=[
                pl.BlockSpec(att.shape, lambda s, p: (0, 0), pipeline_mode=once),
                pl.BlockSpec(mam.shape, lambda s, p: (0, 0), pipeline_mode=once),
                pl.BlockSpec((rows, 2 * rows), lambda s, p: (0, p[0]), pipeline_mode=once),
                pl.BlockSpec((wm.shape[0], 2 * rows), lambda s, p: (0, p[0]), pipeline_mode=once),
            ],
            out_specs=(block, block),
        ),
        out_shape=(
            jax.ShapeDtypeStruct((rows, T), F32), jax.ShapeDtypeStruct((rows, T), BF16)
        ),
        compiler_params=vmem(12),
        name="project",
    )(place, att, mam, wa, wm)


def prepare_kernel(place_ref, *refs):
    z_refs, unscale_ref, rows_ref, inv_ref = refs[:-3], refs[-3], refs[-2], refs[-1]
    chips = len(z_refs) // 2
    pair = unscale_ref.shape[1]
    first = place_ref[1] == 0
    total = jnp.zeros((T, 128), F32)
    for d in range(chips):
        mine, theirs = z_refs[2 * d][...], z_refs[2 * d + 1][...]
        both = jnp.concatenate(
            [jnp.where(first, mine, theirs), jnp.where(first, theirs, mine)], axis=0
        ).T
        chip = lax.rem(place_ref[0] + chips - d, chips)
        rows_ref[:, pl.ds(pl.multiple_of(chip * pair, 128), pair)] = both
        plain = both.astype(F32) * unscale_ref[pl.ds(chip, 1), :]
        square = plain * plain
        for i in range(pair // 128):
            total = total + square[:, 128 * i : 128 * i + 128]
    inv_ref[...] = jnp.broadcast_to(
        lax.rsqrt(jnp.sum(total, axis=1, keepdims=True) / (chips * pair) + EPS), (T, 128)
    )


def prepare(place, blocks, unscale):
    smem = pl.BlockSpec(memory_space=pltpu.SMEM)
    full = pl.BlockSpec(memory_space=pltpu.VMEM)
    return pl.pallas_call(
        prepare_kernel,
        in_specs=[smem] + [full] * (len(blocks) + 1),
        out_shape=(
            jax.ShapeDtypeStruct((T, unscale.size), BF16), jax.ShapeDtypeStruct((T, 128), F32)
        ),
        compiler_params=vmem(14),
        name="prepare",
    )(place, *blocks, unscale)


def activate_kernel(rows_ref, inv_ref, gu_ref, act_ref):
    width = rows_ref.shape[1]
    w = jnp.concatenate(
        [gu_ref[:, 0].reshape(width, 128), gu_ref[:, 1].reshape(width, 128)], axis=1
    )
    both = dot(rows_ref[...], w)
    gate = both[:, 0:128] * inv_ref[...]
    up = both[:, 128:256] * inv_ref[...]
    act_ref[...] = (gate / (1.0 + jnp.exp(-gate)) * up).astype(BF16)


def activate(rows, inv, weights):
    parts, _, height, hidden = weights.shape
    once = pl.Buffered(1)
    return pl.pallas_call(
        activate_kernel,
        grid=(hidden // 128,),
        in_specs=[
            pl.BlockSpec(rows.shape, lambda s: (0, 0), pipeline_mode=once),
            pl.BlockSpec(inv.shape, lambda s: (0, 0), pipeline_mode=once),
            pl.BlockSpec((parts, 2, height, 128), lambda s: (0, 0, 0, s)),
        ],
        out_specs=pl.BlockSpec((T, 128), lambda s: (0, s)),
        out_shape=jax.ShapeDtypeStruct((T, hidden), BF16),
        compiler_params=vmem(16),
        name="activate",
    )(rows, inv, weights)


def down_kernel(place_ref, act_ref, w_ref, own_ref, other_ref):
    half, hidden = own_ref.shape[0], act_ref.shape[1]
    per = w_ref.shape[0] // 2
    act = act_ref[...]
    c = place_ref[1]
    theirs = w_ref[pl.ds(per * (1 - c), per), 0].reshape(half, hidden)
    other_ref[...] = dot(theirs, act, 1, 1).astype(BF16)
    mine = w_ref[pl.ds(per * c, per), 0].reshape(half, hidden)
    own_ref[...] = dot(mine, act, 1, 1)


def down(place, act, weights):
    parts, _, height, hidden = weights.shape
    per = parts // 4
    rows = per * height // 2
    return pl.pallas_call(
        down_kernel,
        grid_spec=pltpu.PrefetchScalarGridSpec(
            num_scalar_prefetch=1,
            grid=(1,),
            in_specs=[
                pl.BlockSpec(act.shape, lambda s, p: (0, 0)),
                pl.BlockSpec((per, 1, height, hidden), lambda s, p: (p[0], 2, 0, 0)),
            ],
            out_specs=(
                pl.BlockSpec((rows, T), lambda s, p: (0, 0)),
                pl.BlockSpec((rows, T), lambda s, p: (0, 0)),
            ),
        ),
        out_shape=(
            jax.ShapeDtypeStruct((rows, T), F32), jax.ShapeDtypeStruct((rows, T), BF16)
        ),
        compiler_params=vmem(14),
        name="down",
    )(place, act, weights)


def behind(value, steps):
    count = lax.axis_size(REQ)
    pairs = [(i, i + steps) for i in range(count) if 0 <= i + steps < count]
    return lax.ppermute(value, REQ, pairs)


def along(value, steps):
    count = lax.axis_size("x")
    return lax.ppermute(value, "x", [(i, (i + steps) % count) for i in range(count)])


def swap(value):
    return lax.ppermute(value, "c", [(0, 1), (1, 0)])


ORDER = (2, 1, 3, 0)


def scatter_sum(block_of, source):
    sent, waiting = [], []

    def send(s, own, other):
        paired = own + other.astype(F32)
        if not s:
            sent.append(paired)
            return paired
        narrow = paired.astype(BF16)
        sent.append(along(narrow, s).astype(F32))
        return narrow

    for s in ORDER:
        own, other = block_of(s, source)
        waiting.append((s, own, swap(other)))
        if s in (1, 3):
            done = [send(*item) for item in waiting][-1]
            source, _ = lax.optimization_barrier((source, done))
            waiting = []
    for item in waiting:
        send(*item)
    return sent[0] + sent[1] + sent[2] + sent[3]


def gather_rows(share):
    got = []
    for d in range(4):
        here = along(share, d) if d else share
        got += [here, swap(here)]
    return got


def group_sum(value):
    paired = value + swap(value)
    return paired + along(paired, 1) + along(paired, 2) + along(paired, 3)


def body(
    hidden, query_heads, key_heads, value_heads, segment_ids, page_table, mamba_conv_input,
    mamba_output_gate, state_input_projection, state_output_projection, discrete_step_size,
    head_decay_rate, skip_gain, mamba_gated_norm_gain, attn_proj, mamba_output_projection,
    mlp_norm_gain, gate_proj, up_proj, down_proj, next_norm_gain,
):
    row_count = query_heads.shape[0]
    head_count = query_heads.shape[1] // HD
    width = hidden.shape[1]
    total_width = mlp_norm_gain.shape[0]
    owner = lax.axis_index("x") * lax.axis_size("c") + lax.axis_index("c")

    x = lax.axis_index("x")
    core = lax.axis_index("c")

    def place(steps):
        return jnp.stack([(x + steps) % 4, core]).astype(jnp.int32)

    stacked_weights = jnp.stack([gate_proj, up_proj, down_proj.T])
    weights = in_hbm(lax.all_gather(stacked_weights, REQ, axis=0, tiled=False))

    seg_row = segment_ids.reshape(1, row_count)
    seg_col = segment_ids.reshape(row_count, 1)
    state, row, col = leaving_state(
        discrete_step_size.T, head_decay_rate.reshape(-1, 1), seg_row, mamba_conv_input,
        state_input_projection,
    )
    near = behind(state, 1)

    q, k, v = query_heads.T, key_heads.T, value_heads.T
    ids = jnp.broadcast_to((segment_ids + 1).astype(BF16)[None, :], (16, row_count))
    kv1 = behind(jnp.concatenate([k, v, ids], axis=0), 1)
    next_q = behind(jnp.concatenate([q, ids], axis=0), -1)

    page_count = page_table.shape[1]

    def to_pages(source):
        return (
            source.reshape(page_count, PAGE, head_count, HD)
            .transpose(2, 0, 1, 3)
            .reshape(head_count, page_count, PAGE * HD)
        )

    stacked = jnp.stack([to_pages(key_heads), to_pages(value_heads)])
    kv_cache = jnp.zeros_like(stacked).at[:, :, page_table[0]].set(stacked)

    own_out, own_lse = attend_own(q, k, v, seg_row, seg_col)
    skip = jnp.repeat(skip_gain, mamba_conv_input.shape[1] // skip_gain.shape[0]).reshape(1, -1)
    local = mamba_local(
        mamba_conv_input, state_input_projection, state_output_projection, row, col, seg_row,
        seg_col, skip,
    )
    waited_col, own_lse, local = lax.optimization_barrier((seg_col, own_lse, local))
    next_out = attend_next(next_q, k, v, kv1, waited_col)
    far_out = behind(next_out, 1)
    state, near, _ = lax.optimization_barrier((state, near, next_out))
    carry = behind(pass_through(state, near), 1)
    gated, squares = mamba_finish(
        in_hbm(local), mamba_output_gate, state_output_projection, col, seg_col, carry
    )
    mam = normalize(gated, group_sum(squares), mamba_gated_norm_gain.reshape(1, -1))
    own_out, mam = lax.optimization_barrier((own_out, mam))
    att = merge(in_hbm(own_out), own_lse, far_out)
    attn_proj, mamba_output_projection = in_hbm(attn_proj), in_hbm(mamba_output_projection)
    mixed = hidden.T.astype(F32) + scatter_sum(
        lambda s, rows: project(place(s), rows, mam, attn_proj, mamba_output_projection), att
    )
    own_gain = lax.dynamic_slice_in_dim(mlp_norm_gain, owner * width, width, 0)
    blocks = gather_rows((mixed * own_gain[:, None]).astype(BF16))
    rows, inv = prepare(place(0), blocks, (1.0 / mlp_norm_gain).reshape(4, -1))
    act = activate(in_hbm(rows), inv, weights)
    new_hidden = (mixed + scatter_sum(lambda s, rows: down(place(s), rows, weights), act)).astype(BF16)
    widened = new_hidden.astype(F32)
    total_sq = group_sum(jnp.sum(widened * widened, axis=0, keepdims=True))
    next_normed = (
        widened * lax.rsqrt(total_sq / total_width + EPS) * next_norm_gain[:, None]
    ).astype(BF16)

    return (new_hidden.T, next_normed.T, kv_cache)


def solution(mesh):
    split = Mesh(mesh.devices.reshape(4, 4, 4, 2), ("z", "y", "x", "c"))
    tokens = P(REQ, MLP)
    return jax.shard_map(
        body,
        mesh=split,
        in_specs=(
            tokens, tokens, tokens, tokens, P(REQ), P(REQ, None), tokens, tokens, P(REQ, None),
            P(REQ, None), tokens, P(MLP), P(MLP), P(MLP), P(MLP, None), P(MLP, None), P(), tokens,
            tokens, P(MLP, REQ), P(MLP),
        ),
        out_specs=(tokens, tokens, P(None, MLP, REQ, None)),
        check_vma=False,
    )
```

```python
import functools
import math

import jax
import jax.numpy as jnp
from jax import lax
from jax.experimental import pallas as pl
from jax.experimental.pallas import tpu as pltpu
from jax.sharding import Mesh
from jax.sharding import PartitionSpec as P

HD = 224
PAGE = 16
EPS = 1e-05
LOG2E = math.log2(math.e)
T = 512
F32 = jnp.float32
BF16 = jnp.bfloat16
REQ = ("z", "y")
MLP = ("x", "c")


def vmem(mib):
    return pltpu.CompilerParams(vmem_limit_bytes=mib << 20)


def in_hbm(value):
    return pltpu.with_memory_space_constraint(value, pltpu.HBM)


def dot(a, b, ca=1, cb=0):
    return lax.dot_general(a, b, (((ca,), (cb,)), ((), ())), preferred_element_type=F32)


def lanes_of(shape):
    return lax.broadcasted_iota(jnp.int32, shape, 1)


def halves(pair, i, rows, base=0):
    low = jnp.broadcast_to(pair[:, base + 2 * i : base + 2 * i + 1], (rows, 128))
    high = jnp.broadcast_to(pair[:, base + 2 * i + 1 : base + 2 * i + 2], (rows, 128))
    return jnp.where(lanes_of((rows, 128)) < 64, low, high)


def state_kernel(dt_ref, rate_ref, seg_ref, x_ref, b_ref, state_ref, row_ref, col_ref, tmp_ref):
    heads = dt_ref.shape[0]
    tiles = x_ref.shape[1] // 128
    tmp_ref[...] = jnp.zeros_like(tmp_ref)
    tmp_ref[0:heads, :] = dt_ref[...] * (rate_ref[...] * -LOG2E)
    tmp_ref[16:32, :] = jnp.ones((16, T), F32)
    tmp_ref[16 : 16 + heads, :] = dt_ref[...]
    run = tmp_ref[0:16, :]
    lane = lanes_of((16, T))
    shift = 1
    while shift < T:
        run = run + jnp.where(lane >= shift, pltpu.roll(run, shift, 1), 0.0)
        shift *= 2
    row = run - jnp.log2(tmp_ref[16:32, :])
    row_ref[...] = row
    last = jnp.sum(jnp.where(lane == T - 1, run, 0.0), axis=1, keepdims=True)
    seg = seg_ref[...]
    tail = jnp.where(seg == jnp.max(seg), 1.0, 0.0)
    tmp_ref[0:16, :] = run
    tmp_ref[16:32, :] = jnp.exp2(last - row) * tail
    col = tmp_ref[...].T
    col_ref[...] = col
    b_rows = b_ref[...].astype(F32).T.astype(BF16)
    for i in range(tiles):
        cut = slice(128 * i, 128 * i + 128)
        weighted = (x_ref[:, cut].astype(F32) * halves(col, i, T, 16)).astype(BF16)
        both = dot(b_rows, weighted)
        kept = jnp.where(lanes_of((64, 128)) < 64, both[0:64], both[64:128])
        state_ref[0:64, cut] = kept.astype(BF16)
        gone = jnp.exp2(halves(col[T - 8 : T], i, 8))[7:8]
        final = jnp.broadcast_to((jnp.max(seg) + 1).astype(F32), (8, 128))
        state_ref[64:80, cut] = jnp.concatenate(
            [jnp.broadcast_to(gone, (8, 128)), final], axis=0
        ).astype(BF16)


def leaving_state(dt_rows, rate, seg_row, x, b):
    width = x.shape[1]
    return pl.pallas_call(
        state_kernel,
        out_shape=(
            jax.ShapeDtypeStruct((80, width), BF16),
            jax.ShapeDtypeStruct((16, T), F32),
            jax.ShapeDtypeStruct((T, 128), F32),
        ),
        scratch_shapes=[pltpu.VMEM((128, T), F32)],
        compiler_params=vmem(12),
        name="leaving_state",
    )(dt_rows, rate, seg_row, x, b)


def through_kernel(state_ref, near_ref, out_ref):
    tail = state_ref[64:80, :].astype(F32)
    before = near_ref[64:80, :].astype(F32)
    passes = jnp.where(tail[8:9] == before[8:9], tail[0:1], 0.0)
    out_ref[0:64, :] = (
        state_ref[0:64, :].astype(F32) + passes * near_ref[0:64, :].astype(F32)
    ).astype(BF16)
    out_ref[64:80, :] = state_ref[64:80, :]


def pass_through(state, near):
    return pl.pallas_call(
        through_kernel,
        out_shape=jax.ShapeDtypeStruct(state.shape, BF16),
        compiler_params=vmem(4),
        name="pass_through",
    )(state, near)


HALF = T // 2


def local_kernel(x_ref, b_ref, c_ref, row_ref, col_ref, segr_ref, segc_ref, skip_ref, out_ref, inner_ref):
    tiles = x_ref.shape[1] // 128
    b = b_ref[...]
    c = c_ref[...]
    live = (segc_ref[...] == segr_ref[...]) & (
        lax.broadcasted_iota(jnp.int32, (T, T), 0) >= lanes_of((T, T))
    )
    group = lanes_of((T, 128)) < 64
    for g in range(2):
        own = jnp.where(group == (g == 0), c, jnp.zeros_like(c))
        inner_ref[g] = jnp.where(live, dot(own, b, 1, 1), 0.0)
    col = col_ref[...]
    lane = lanes_of((T, 128))
    low = lanes_of((HALF, 128)) < 64

    def tile(i, _):
        cut = pl.ds(pl.multiple_of(i * 128, 128), 128)
        decays = [
            jnp.sum(jnp.where(lane == 2 * i + g, col, 0.0), axis=1, keepdims=True) for g in range(2)
        ]
        rows_of = [row_ref[pl.ds(2 * i + g, 1), :] for g in range(2)]
        for k in range(2):
            rows = slice(HALF * k, HALF * k + HALF)
            upto = HALF * (k + 1)
            parts = []
            for g in range(2):
                power = jnp.minimum(decays[g][rows] - rows_of[g][:, 0:upto], 126.0)
                mixing = (jnp.exp2(power) * inner_ref[g, rows, 0:upto]).astype(BF16)
                parts.append(dot(mixing, x_ref[0:upto, cut]))
            y = jnp.where(low, parts[0], parts[1])
            out_ref[rows, cut] = y + skip_ref[:, cut] * x_ref[rows, cut].astype(F32)
        return 0

    lax.fori_loop(0, tiles, tile, 0)


def mamba_local(x, b, c, row, col, seg_row, seg_col, skip):
    return pl.pallas_call(
        local_kernel,
        out_shape=jax.ShapeDtypeStruct(x.shape, F32),
        scratch_shapes=[pltpu.VMEM((2, T, T), F32)],
        compiler_params=vmem(14),
        name="mamba_local",
    )(x, b, c, row, col, seg_row, seg_col, skip)


def finish_kernel(y_ref, z_ref, c_ref, col_ref, segc_ref, carry_ref, out_ref, sq_ref):
    tiles = y_ref.shape[1] // 128
    c = c_ref[...]
    last = jnp.max(carry_ref[64:80, 0:128].astype(F32)[8:16])
    enters = segc_ref[...].astype(F32) + 1.0 == last
    entry = jnp.where(enters, jnp.exp2(col_ref[...]), 0.0)
    first = lanes_of((64, 128)) < 64
    total = jnp.zeros((T, 128), F32)
    for i in range(tiles):
        cut = slice(128 * i, 128 * i + 128)
        carry = carry_ref[0:64, cut]
        nothing = jnp.zeros_like(carry)
        spread_state = jnp.concatenate(
            [jnp.where(first, carry, nothing), jnp.where(first, nothing, carry)], axis=0
        )
        y = y_ref[:, cut] + halves(entry, i, T) * dot(c, spread_state)
        z = z_ref[:, cut].astype(F32)
        gated = y * (z / (1.0 + jnp.exp(-z)))
        out_ref[:, cut] = gated
        total = total + gated * gated
    turned = total.T
    even = jnp.sum(turned[0:64], axis=0, keepdims=True)
    odd = jnp.sum(turned[64:128], axis=0, keepdims=True)
    sq_ref[...] = jnp.concatenate([even, odd], axis=0)


def mamba_finish(y, z, c, col, seg_col, carry):
    return pl.pallas_call(
        finish_kernel,
        out_shape=(jax.ShapeDtypeStruct(y.shape, F32), jax.ShapeDtypeStruct((2, T), F32)),
        compiler_params=vmem(14),
        name="mamba_finish",
    )(y, z, c, col, seg_col, carry)


def normalize_kernel(gated_ref, sq_ref, gain_ref, out_ref):
    tiles = gated_ref.shape[1] // 128
    inverse = lax.rsqrt(sq_ref[...] / (tiles * 64 * 8) + EPS)
    spread = jnp.concatenate(
        [jnp.broadcast_to(inverse[0:1], (64, T)), jnp.broadcast_to(inverse[1:2], (64, T))], axis=0
    )
    for i in range(tiles):
        cut = slice(128 * i, 128 * i + 128)
        out_ref[cut, :] = ((gated_ref[:, cut] * gain_ref[:, cut]).T * spread).astype(BF16)


def normalize(gated, squares, gain):
    return pl.pallas_call(
        normalize_kernel,
        out_shape=jax.ShapeDtypeStruct(gated.shape[::-1], BF16),
        compiler_params=vmem(10),
        name="normalize",
    )(gated, squares, gain)


NONE = -1e30


def softmax_of(parts, values):
    top = parts[0]
    for part in parts[1:]:
        top = jnp.maximum(top, part)
    top = jnp.maximum(jnp.max(top, axis=0, keepdims=True), NONE)
    raised = [jnp.exp2(part - top) for part in parts]
    total = sum(raised)
    total = jnp.sum(total, axis=0, keepdims=True)
    some = total > 0.0
    safe = jnp.where(some, total, 1.0)
    share = jnp.where(some, 1.0 / safe, 0.0)
    out = sum(dot(value, (part * share).astype(BF16)) for part, value in zip(raised, values))
    return out, jnp.where(some, top + jnp.log2(safe), NONE)


def own_kernel(q_ref, k_ref, v_ref, segr_ref, segc_ref, out_ref, lse_ref):
    scale = LOG2E / math.sqrt(HD)
    mask = (segc_ref[...] == segr_ref[...]) & (
        lax.broadcasted_iota(jnp.int32, (T, T), 0) <= lanes_of((T, T))
    )
    lse_ref[...] = jnp.zeros_like(lse_ref)
    for h in range(q_ref.shape[0] // HD):
        at = slice(HD * h, HD * h + HD)
        part = jnp.where(mask, dot(k_ref[at, :], q_ref[at, :], 0, 0) * scale, -jnp.inf)
        out_ref[at, :], lse_ref[h : h + 1, :] = softmax_of([part], [v_ref[at, :]])


def attend_own(q, k, v, seg_row, seg_col):
    return pl.pallas_call(
        own_kernel,
        out_shape=(jax.ShapeDtypeStruct(q.shape, F32), jax.ShapeDtypeStruct((8, T), F32)),
        compiler_params=vmem(12),
        name="attend_own",
    )(q, k, v, seg_row, seg_col)


def next_kernel(q_ref, k_ref, v_ref, kv_ref, segc_ref, out_ref):
    width = k_ref.shape[0]
    scale = LOG2E / math.sqrt(HD)
    wanted = q_ref[width : width + 16, :].astype(F32)[0:1]
    ids = kv_ref[2 * width : 2 * width + 16, :].astype(F32)[0:8]
    before = jnp.concatenate([ids] * 16, axis=0).T[:, 0:1]
    masks = (segc_ref[...].astype(F32) + 1.0 == wanted, before == wanted)
    rows = []
    for h in range(width // HD):
        at = slice(HD * h, HD * h + HD)
        theirs = slice(width + HD * h, width + HD * h + HD)
        keys, values = (k_ref[at, :], kv_ref[at, :]), (v_ref[at, :], kv_ref[theirs, :])
        parts = [
            jnp.where(mask, dot(key, q_ref[at, :], 0, 0) * scale, -jnp.inf)
            for mask, key in zip(masks, keys)
        ]
        out, lse = softmax_of(parts, values)
        out_ref[at, :] = out.astype(BF16)
        for _ in range(3):
            rows.append(lse.astype(BF16).astype(F32))
            lse = lse - rows[-1]
    rows.append(jnp.ones((16 - len(rows), T), F32))
    out_ref[width : width + 16, :] = jnp.concatenate(rows, axis=0).astype(BF16)


def attend_next(q, k, v, kv, seg_col):
    return pl.pallas_call(
        next_kernel,
        out_shape=jax.ShapeDtypeStruct(q.shape, BF16),
        compiler_params=vmem(14),
        name="attend_next",
    )(q, k, v, kv, seg_col)


def merge_kernel(out_ref, lse_ref, far_ref, rows_ref):
    width = out_ref.shape[0]
    stats = far_ref[width : width + 16, :].astype(F32)
    given = stats[15:16] > 0.0
    merged = []
    for h in range(width // HD):
        at = slice(HD * h, HD * h + HD)
        lse = stats[3 * h : 3 * h + 1] + stats[3 * h + 1 : 3 * h + 2] + stats[3 * h + 2 : 3 * h + 3]
        lse = jnp.where(given, lse, NONE)
        own = lse_ref[h : h + 1, :]
        top = jnp.maximum(lse, own)
        near, far = jnp.exp2(own - top), jnp.exp2(lse - top)
        total = near + far
        merged.append(
            out_ref[at, :] * (near / total) + far_ref[at, :].astype(F32) * (far / total)
        )
    rows_ref[...] = jnp.concatenate(merged, axis=0).astype(BF16)


def merge(out, lse, far):
    return pl.pallas_call(
        merge_kernel,
        out_shape=jax.ShapeDtypeStruct(out.shape, BF16),
        compiler_params=vmem(8),
        name="merge",
    )(out, lse, far)


ORDER = (2, 1, 3, 0)


def send_out(step, refs, own_s, other_s, sems):
    for k in range(len(ORDER)):
        pair = (
            pltpu.make_async_copy(own_s.at[k], refs[2 * k], sems.at[0, k]),
            pltpu.make_async_copy(other_s.at[k], refs[2 * k + 1], sems.at[1, k]),
        )

        @pl.when(step == k)
        def _(pair=pair):
            for copy in pair:
                copy.start()

    @pl.when(step == len(ORDER) - 1)
    def _():
        for k in range(len(ORDER)):
            pltpu.make_async_copy(own_s.at[k], refs[2 * k], sems.at[0, k]).wait()
            pltpu.make_async_copy(other_s.at[k], refs[2 * k + 1], sems.at[1, k]).wait()


def block_outputs(rows):
    count = len(ORDER)
    raw = pl.BlockSpec(memory_space=pl.ANY)
    pair = [jax.ShapeDtypeStruct((rows, T), F32), jax.ShapeDtypeStruct((rows, T), BF16)]
    scratch = [
        pltpu.VMEM((count, rows, T), F32),
        pltpu.VMEM((count, rows, T), BF16),
        pltpu.SemaphoreType.DMA((2, count)),
    ]
    return pair * count, [raw] * (2 * count), scratch


def project_kernel(place_ref, att_ref, mam_ref, wa_ref, wm_ref, *refs):
    outs, (own_s, other_s, sems) = refs[:-3], refs[-3:]
    step = pl.program_id(0)
    half = own_s.shape[1]
    out = dot(wa_ref[...], att_ref[...], 0, 0) + dot(wm_ref[...], mam_ref[...], 0, 0)
    first = place_ref[len(ORDER)] == 0
    own_s[step] = jnp.where(first, out[0:half], out[half:])
    other_s[step] = jnp.where(first, out[half:], out[0:half]).astype(BF16)
    send_out(step, outs, own_s, other_s, sems)


def project(place, att, mam, wa, wm):
    rows = wa.shape[0]
    once = pl.Buffered(1)
    shapes, specs, scratch = block_outputs(rows)
    return pl.pallas_call(
        project_kernel,
        grid_spec=pltpu.PrefetchScalarGridSpec(
            num_scalar_prefetch=1,
            grid=(len(ORDER),),
            in_specs=[
                pl.BlockSpec(att.shape, lambda s, p: (0, 0), pipeline_mode=once),
                pl.BlockSpec(mam.shape, lambda s, p: (0, 0), pipeline_mode=once),
                pl.BlockSpec((rows, 2 * rows), lambda s, p: (0, p[s])),
                pl.BlockSpec((wm.shape[0], 2 * rows), lambda s, p: (0, p[s])),
            ],
            out_specs=specs,
            scratch_shapes=scratch,
        ),
        out_shape=shapes,
        compiler_params=vmem(20),
        name="project",
    )(place, att, mam, wa, wm)


def prepare_kernel(place_ref, *refs):
    z_refs, unscale_ref, rows_ref, inv_ref = refs[:-3], refs[-3], refs[-2], refs[-1]
    chips, pair = unscale_ref.shape
    mine = [ref[...] for ref in z_refs[0::2]]
    theirs = [ref[...] for ref in z_refs[1::2]]
    mine, theirs = (
        [b[0], b[1], jnp.concatenate([b[2], b[3]], axis=0), b[4]] for b in (mine, theirs)
    )
    first = place_ref[1] == 0
    total = jnp.zeros((T, 128), F32)
    for d in range(chips):
        both = jnp.concatenate(
            [jnp.where(first, mine[d], theirs[d]), jnp.where(first, theirs[d], mine[d])], axis=0
        ).T
        chip = lax.rem(place_ref[0] + chips - d, chips)
        rows_ref[:, pl.ds(pl.multiple_of(chip * pair, 128), pair)] = both
        plain = both.astype(F32) * unscale_ref[pl.ds(chip, 1), :]
        square = plain * plain
        for i in range(pair // 128):
            total = total + square[:, 128 * i : 128 * i + 128]
    inv_ref[...] = jnp.broadcast_to(
        lax.rsqrt(jnp.sum(total, axis=1, keepdims=True) / (chips * pair) + EPS), (T, 128)
    )


def prepare(place, blocks, unscale):
    smem = pl.BlockSpec(memory_space=pltpu.SMEM)
    full = pl.BlockSpec(memory_space=pltpu.VMEM)
    return pl.pallas_call(
        prepare_kernel,
        in_specs=[smem] + [full] * (len(blocks) + 1),
        out_shape=(
            jax.ShapeDtypeStruct((T, unscale.size), BF16), jax.ShapeDtypeStruct((T, 128), F32)
        ),
        compiler_params=vmem(14),
        name="prepare",
    )(place, *blocks, unscale)


def mlp_kernel(place_ref, rows_ref, inv_ref, gu_ref, down_ref, *refs):
    outs, (act_s, own_s, other_s, sems) = refs[:-4], refs[-4:]
    half, hidden = own_s.shape[1], act_s.shape[1]
    first = hidden // 128
    step = pl.program_id(0)

    @pl.when(step < first)
    def _():
        width = rows_ref.shape[1]
        w = jnp.concatenate(
            [gu_ref[:, 0].reshape(width, 128), gu_ref[:, 1].reshape(width, 128)], axis=1
        )
        both = dot(rows_ref[...], w)
        gate = both[:, 0:128] * inv_ref[...]
        up = both[:, 128:256] * inv_ref[...]
        act_s[:, pl.ds(pl.multiple_of(step * 128, 128), 128)] = (
            gate / (1.0 + jnp.exp(-gate)) * up
        ).astype(BF16)

    @pl.when(step >= first)
    def _():
        k = step - first
        out = dot(down_ref[:, 0].reshape(2 * half, hidden), act_s[...], 1, 1)
        lower = place_ref[len(ORDER)] == 0
        own_s[k] = jnp.where(lower, out[0:half], out[half:])
        other_s[k] = jnp.where(lower, out[half:], out[0:half]).astype(BF16)

    send_out(step - first, outs, own_s, other_s, sems)


def mlp(place, rows, inv, weights):
    parts, _, height, hidden = weights.shape
    once = pl.Buffered(1)
    first = hidden // 128
    count = len(ORDER)
    per = parts // count
    shapes, specs, scratch = block_outputs(per * height // 2)
    return pl.pallas_call(
        mlp_kernel,
        grid_spec=pltpu.PrefetchScalarGridSpec(
            num_scalar_prefetch=1,
            grid=(first + count,),
            in_specs=[
                pl.BlockSpec(rows.shape, lambda s, p: (0, 0), pipeline_mode=once),
                pl.BlockSpec(inv.shape, lambda s, p: (0, 0), pipeline_mode=once),
                pl.BlockSpec(
                    (parts, 2, height, 128), lambda s, p: (0, 0, 0, jnp.minimum(s, first - 1))
                ),
                pl.BlockSpec(
                    (per, 1, height, hidden), lambda s, p: (p[jnp.maximum(s - first, 0)], 2, 0, 0)
                ),
            ],
            out_specs=specs,
            scratch_shapes=[pltpu.VMEM((T, hidden), BF16), *scratch],
        ),
        out_shape=shapes,
        compiler_params=vmem(26),
        name="mlp",
    )(place, rows, inv, weights, weights)


def pages_kernel(table_ref, k_ref, v_ref, out_ref):
    pages = out_ref.shape[2]
    row = lax.broadcasted_iota(jnp.int32, (T, T), 0)
    chosen = (table_ref[...] == lax.rem(row, pages)) & (
        lax.rem(lanes_of((T, T)), PAGE) == row // pages
    )
    chosen = jnp.where(chosen, 1.0, 0.0).astype(BF16)
    for i, ref in enumerate((k_ref, v_ref)):
        for h in range(ref.shape[0] // HD):
            tokens = dot(chosen, ref[HD * h : HD * h + HD, :], 1, 1).astype(BF16)
            for j in range(PAGE):
                out_ref[i, h, :, HD * j : HD * j + HD] = tokens[pages * j : pages * j + pages]


def cache_pages(table, k, v):
    heads, pages = k.shape[0] // HD, table.shape[1]
    return pl.pallas_call(
        pages_kernel,
        out_shape=jax.ShapeDtypeStruct((2, heads, pages, PAGE * HD), BF16),
        compiler_params=vmem(10),
        name="cache_pages",
    )(jnp.repeat(table, PAGE, axis=1), k, v)


def stack_kernel(a_ref, b_ref, c_ref, out_ref, held_ref, sems):
    refs = (a_ref, b_ref, c_ref)
    loads = [pltpu.make_async_copy(r, held_ref.at[i], sems.at[0, i]) for i, r in enumerate(refs)]
    saves = [
        pltpu.make_async_copy(held_ref.at[i], out_ref.at[i], sems.at[1, i]) for i in range(len(refs))
    ]
    for load in loads:
        load.start()
    for load, save in zip(loads, saves):
        load.wait()
        save.start()
    for save in saves:
        save.wait()


def stack_three(a, b, c):
    raw = pl.BlockSpec(memory_space=pl.ANY)
    return pl.pallas_call(
        stack_kernel,
        in_specs=[raw, raw, raw],
        out_specs=raw,
        out_shape=jax.ShapeDtypeStruct((3, *a.shape), a.dtype),
        scratch_shapes=[pltpu.VMEM((3, *a.shape), a.dtype), pltpu.SemaphoreType.DMA((2, 3))],
        compiler_params=vmem(4),
        name="stack_three",
    )(in_hbm(a), in_hbm(b), in_hbm(c))


def behind(value, steps):
    count = lax.axis_size(REQ)
    pairs = [(i, i + steps) for i in range(count) if 0 <= i + steps < count]
    return lax.ppermute(value, REQ, pairs)


def along(value, steps):
    count = lax.axis_size("x")
    return lax.ppermute(value, "x", [(i, (i + steps) % count) for i in range(count)])


def swap(value):
    return lax.ppermute(value, "c", [(0, 1), (1, 0)])


def add_kernel(own_ref, other_ref, *refs, top):
    out_ref = refs[-1]
    half = out_ref.shape[0] // 2
    total = own_ref[...] + other_ref[...].astype(F32)
    first, second = total[0:half], total[half:]
    extra = refs[0][...].astype(F32)
    out_ref[0:half, :] = (first + extra if top else first).astype(BF16)
    out_ref[half:, :] = (second if top else second + extra).astype(BF16)


def add_up(own, other, extra, top):
    return pl.pallas_call(
        functools.partial(add_kernel, top=top),
        out_shape=jax.ShapeDtypeStruct(own.shape, BF16),
        compiler_params=vmem(6),
        name="add_up",
    )(own, other, extra)


def halves_kernel(own_ref, other_ref, first_ref, second_ref):
    half = first_ref.shape[0]
    total = (own_ref[...] + other_ref[...].astype(F32)).astype(BF16)
    first_ref[...] = total[0:half]
    second_ref[...] = total[half:]


def add_halves(own, other):
    half = jax.ShapeDtypeStruct((own.shape[0] // 2, own.shape[1]), BF16)
    return pl.pallas_call(
        halves_kernel, out_shape=(half, half), compiler_params=vmem(6), name="add_halves"
    )(own, other)


def scatter_sum(blocks, base):
    own2, other2, own1, other1, own3, other3, own0, other0 = blocks
    up, low = add_halves(own2, swap(other2))
    up, low = along(up, 1), along(low, 3)
    other1, other3, other0 = swap(other1), swap(other3), swap(other0)
    from_left = along(add_up(own1, other1, up, True), 1)
    from_right = along(add_up(own3, other3, low, False), 3)
    base = lax.optimization_barrier(base + own0 + other0.astype(F32))
    return base + from_left.astype(F32) + from_right.astype(F32)


def gather_rows(share):
    half = share.shape[0] // 2
    left, right = along(share, 1), along(share, 3)
    first, second = along(left[:half], 1), along(right[half:], 3)
    got = []
    for block in (share, left, first, second, right):
        got += [block, swap(block)]
    return got


def group_sum(value):
    paired = value + swap(value)
    return paired + along(paired, 1) + along(paired, 2) + along(paired, 3)


def body(
    hidden, query_heads, key_heads, value_heads, segment_ids, page_table, mamba_conv_input,
    mamba_output_gate, state_input_projection, state_output_projection, discrete_step_size,
    head_decay_rate, skip_gain, mamba_gated_norm_gain, attn_proj, mamba_output_projection,
    mlp_norm_gain, gate_proj, up_proj, down_proj, next_norm_gain,
):
    row_count = query_heads.shape[0]
    width = hidden.shape[1]
    total_width = mlp_norm_gain.shape[0]
    owner = lax.axis_index("x") * lax.axis_size("c") + lax.axis_index("c")

    x = lax.axis_index("x")
    core = lax.axis_index("c")

    place = jnp.stack([(x + steps) % 4 for steps in ORDER] + [core]).astype(jnp.int32)

    stacked_weights = stack_three(gate_proj, up_proj, down_proj.T)
    weights = in_hbm(lax.all_gather(stacked_weights, REQ, axis=0, tiled=False))

    seg_row = segment_ids.reshape(1, row_count)
    seg_col = segment_ids.reshape(row_count, 1)
    state, row, col = leaving_state(
        discrete_step_size.T, head_decay_rate.reshape(-1, 1), seg_row, mamba_conv_input,
        state_input_projection,
    )
    near = behind(state, 1)

    q, k, v = query_heads.T, key_heads.T, value_heads.T
    ids = jnp.broadcast_to((segment_ids + 1).astype(BF16)[None, :], (16, row_count))
    kv1 = behind(jnp.concatenate([k, v, ids], axis=0), 1)
    next_q = behind(jnp.concatenate([q, ids], axis=0), -1)

    kv_cache = cache_pages(page_table, k, v)
    own_out, own_lse = attend_own(q, k, v, seg_row, seg_col)
    skip = jnp.repeat(skip_gain, mamba_conv_input.shape[1] // skip_gain.shape[0]).reshape(1, -1)
    local = mamba_local(
        mamba_conv_input, state_input_projection, state_output_projection, row, col, seg_row,
        seg_col, skip,
    )
    waited_col, own_lse, local, kv_cache = lax.optimization_barrier(
        (seg_col, own_lse, local, kv_cache)
    )
    next_out = attend_next(next_q, k, v, kv1, waited_col)
    far_out = behind(next_out, 1)
    state, near, _ = lax.optimization_barrier((state, near, next_out))
    carry = behind(pass_through(state, near), 1)
    gated, squares = mamba_finish(
        in_hbm(local), mamba_output_gate, state_output_projection, col, seg_col, carry
    )
    mam = normalize(gated, group_sum(squares), mamba_gated_norm_gain.reshape(1, -1))
    own_out, mam = lax.optimization_barrier((own_out, mam))
    att = merge(in_hbm(own_out), own_lse, far_out)
    attn_proj, mamba_output_projection = in_hbm(attn_proj), in_hbm(mamba_output_projection)
    mixed = scatter_sum(
        project(place, att, mam, attn_proj, mamba_output_projection), hidden.T.astype(F32)
    )
    own_gain = lax.dynamic_slice_in_dim(mlp_norm_gain, owner * width, width, 0)
    blocks = gather_rows((mixed * own_gain[:, None]).astype(BF16))
    here = jnp.stack([x, core]).astype(jnp.int32)
    rows, inv = prepare(here, blocks, (1.0 / mlp_norm_gain).reshape(4, -1))
    new_hidden = scatter_sum(mlp(place, in_hbm(rows), inv, weights), mixed).astype(BF16)
    widened = new_hidden.astype(F32)
    total_sq = group_sum(jnp.sum(widened * widened, axis=0, keepdims=True))
    next_normed = (
        widened * lax.rsqrt(total_sq / total_width + EPS) * next_norm_gain[:, None]
    ).astype(BF16)

    return (new_hidden.T, next_normed.T, kv_cache)


def solution(mesh):
    split = Mesh(mesh.devices.reshape(4, 4, 4, 2), ("z", "y", "x", "c"))
    tokens = P(REQ, MLP)
    return jax.shard_map(
        body,
        mesh=split,
        in_specs=(
            tokens, tokens, tokens, tokens, P(REQ), P(REQ, None), tokens, tokens, P(REQ, None),
            P(REQ, None), tokens, P(MLP), P(MLP), P(MLP), P(MLP, None), P(MLP, None), P(), tokens,
            tokens, P(MLP, REQ), P(MLP),
        ),
        out_specs=(tokens, tokens, P(None, MLP, REQ, None)),
        check_vma=False,
    )
```

```python
import functools
import math

import jax
import jax.numpy as jnp
from jax import lax
from jax.experimental import pallas as pl
from jax.experimental.pallas import tpu as pltpu
from jax.sharding import Mesh
from jax.sharding import PartitionSpec as P

HD = 224
PAGE = 16
EPS = 1e-05
LOG2E = math.log2(math.e)
T = 512
F32 = jnp.float32
BF16 = jnp.bfloat16
REQ = ("z", "y")
MLP = ("x", "c")


def vmem(mib):
    return pltpu.CompilerParams(vmem_limit_bytes=mib << 20)


def in_hbm(value):
    return pltpu.with_memory_space_constraint(value, pltpu.HBM)


def dot(a, b, ca=1, cb=0):
    return lax.dot_general(a, b, (((ca,), (cb,)), ((), ())), preferred_element_type=F32)


def lanes_of(shape):
    return lax.broadcasted_iota(jnp.int32, shape, 1)


def halves(pair, i, rows, base=0):
    low = jnp.broadcast_to(pair[:, base + 2 * i : base + 2 * i + 1], (rows, 128))
    high = jnp.broadcast_to(pair[:, base + 2 * i + 1 : base + 2 * i + 2], (rows, 128))
    return jnp.where(lanes_of((rows, 128)) < 64, low, high)


def state_kernel(dt_ref, rate_ref, seg_ref, x_ref, b_ref, state_ref, row_ref, col_ref, tmp_ref):
    heads = dt_ref.shape[0]
    tiles = x_ref.shape[1] // 128
    tmp_ref[...] = jnp.zeros_like(tmp_ref)
    tmp_ref[0:heads, :] = dt_ref[...] * (rate_ref[...] * -LOG2E)
    tmp_ref[16:32, :] = jnp.ones((16, T), F32)
    tmp_ref[16 : 16 + heads, :] = dt_ref[...]
    run = tmp_ref[0:16, :]
    lane = lanes_of((16, T))
    shift = 1
    while shift < T:
        run = run + jnp.where(lane >= shift, pltpu.roll(run, shift, 1), 0.0)
        shift *= 2
    row = run - jnp.log2(tmp_ref[16:32, :])
    row_ref[...] = row
    last = jnp.sum(jnp.where(lane == T - 1, run, 0.0), axis=1, keepdims=True)
    seg = seg_ref[...]
    tail = jnp.where(seg == jnp.max(seg), 1.0, 0.0)
    tmp_ref[0:16, :] = run
    tmp_ref[16:32, :] = jnp.exp2(last - row) * tail
    col = tmp_ref[...].T
    col_ref[...] = col
    b_rows = b_ref[...].astype(F32).T.astype(BF16)
    for i in range(tiles):
        cut = slice(128 * i, 128 * i + 128)
        weighted = (x_ref[:, cut].astype(F32) * halves(col, i, T, 16)).astype(BF16)
        both = dot(b_rows, weighted)
        kept = jnp.where(lanes_of((64, 128)) < 64, both[0:64], both[64:128])
        state_ref[0:64, cut] = kept.astype(BF16)
        gone = jnp.exp2(halves(col[T - 8 : T], i, 8))[7:8]
        final = jnp.broadcast_to((jnp.max(seg) + 1).astype(F32), (8, 128))
        state_ref[64:80, cut] = jnp.concatenate(
            [jnp.broadcast_to(gone, (8, 128)), final], axis=0
        ).astype(BF16)


def leaving_state(dt_rows, rate, seg_row, x, b):
    width = x.shape[1]
    return pl.pallas_call(
        state_kernel,
        out_shape=(
            jax.ShapeDtypeStruct((80, width), BF16),
            jax.ShapeDtypeStruct((16, T), F32),
            jax.ShapeDtypeStruct((T, 128), F32),
        ),
        scratch_shapes=[pltpu.VMEM((128, T), F32)],
        compiler_params=vmem(12),
        name="leaving_state",
    )(dt_rows, rate, seg_row, x, b)


def through_kernel(state_ref, near_ref, out_ref):
    tail = state_ref[64:80, :].astype(F32)
    before = near_ref[64:80, :].astype(F32)
    passes = jnp.where(tail[8:9] == before[8:9], tail[0:1], 0.0)
    out_ref[0:64, :] = (
        state_ref[0:64, :].astype(F32) + passes * near_ref[0:64, :].astype(F32)
    ).astype(BF16)
    out_ref[64:80, :] = state_ref[64:80, :]


def pass_through(state, near):
    return pl.pallas_call(
        through_kernel,
        out_shape=jax.ShapeDtypeStruct(state.shape, BF16),
        compiler_params=vmem(4),
        name="pass_through",
    )(state, near)


HALF = T // 2


def local_kernel(x_ref, b_ref, c_ref, row_ref, col_ref, segr_ref, segc_ref, skip_ref, out_ref, inner_ref):
    tiles = x_ref.shape[1] // 128
    b = b_ref[...]
    c = c_ref[...]
    live = (segc_ref[...] == segr_ref[...]) & (
        lax.broadcasted_iota(jnp.int32, (T, T), 0) >= lanes_of((T, T))
    )
    group = lanes_of((T, 128)) < 64
    for g in range(2):
        own = jnp.where(group == (g == 0), c, jnp.zeros_like(c))
        inner_ref[g] = jnp.where(live, dot(own, b, 1, 1), 0.0)
    col = col_ref[...]
    lane = lanes_of((T, 128))
    low = lanes_of((HALF, 128)) < 64

    def tile(i, _):
        cut = pl.ds(pl.multiple_of(i * 128, 128), 128)
        decays = [
            jnp.sum(jnp.where(lane == 2 * i + g, col, 0.0), axis=1, keepdims=True) for g in range(2)
        ]
        rows_of = [row_ref[pl.ds(2 * i + g, 1), :] for g in range(2)]
        for k in range(2):
            rows = slice(HALF * k, HALF * k + HALF)
            upto = HALF * (k + 1)
            parts = []
            for g in range(2):
                power = jnp.minimum(decays[g][rows] - rows_of[g][:, 0:upto], 126.0)
                mixing = (jnp.exp2(power) * inner_ref[g, rows, 0:upto]).astype(BF16)
                parts.append(dot(mixing, x_ref[0:upto, cut]))
            y = jnp.where(low, parts[0], parts[1])
            out_ref[rows, cut] = y + skip_ref[:, cut] * x_ref[rows, cut].astype(F32)
        return 0

    lax.fori_loop(0, tiles, tile, 0)


def mamba_local(x, b, c, row, col, seg_row, seg_col, skip):
    return pl.pallas_call(
        local_kernel,
        out_shape=jax.ShapeDtypeStruct(x.shape, F32),
        scratch_shapes=[pltpu.VMEM((2, T, T), F32)],
        compiler_params=vmem(14),
        name="mamba_local",
    )(x, b, c, row, col, seg_row, seg_col, skip)


def finish_kernel(y_ref, z_ref, c_ref, col_ref, segc_ref, carry_ref, out_ref, sq_ref):
    tiles = y_ref.shape[1] // 128
    c = c_ref[...]
    last = jnp.max(carry_ref[64:80, 0:128].astype(F32)[8:16])
    enters = segc_ref[...].astype(F32) + 1.0 == last
    entry = jnp.where(enters, jnp.exp2(col_ref[...]), 0.0)
    first = lanes_of((64, 128)) < 64
    total = jnp.zeros((T, 128), F32)
    for i in range(tiles):
        cut = slice(128 * i, 128 * i + 128)
        carry = carry_ref[0:64, cut]
        nothing = jnp.zeros_like(carry)
        spread_state = jnp.concatenate(
            [jnp.where(first, carry, nothing), jnp.where(first, nothing, carry)], axis=0
        )
        y = y_ref[:, cut] + halves(entry, i, T) * dot(c, spread_state)
        z = z_ref[:, cut].astype(F32)
        gated = y * (z / (1.0 + jnp.exp(-z)))
        out_ref[:, cut] = gated
        total = total + gated * gated
    turned = total.T
    even = jnp.sum(turned[0:64], axis=0, keepdims=True)
    odd = jnp.sum(turned[64:128], axis=0, keepdims=True)
    sq_ref[...] = jnp.concatenate([even, odd], axis=0)


def mamba_finish(y, z, c, col, seg_col, carry):
    return pl.pallas_call(
        finish_kernel,
        out_shape=(jax.ShapeDtypeStruct(y.shape, F32), jax.ShapeDtypeStruct((2, T), F32)),
        compiler_params=vmem(14),
        name="mamba_finish",
    )(y, z, c, col, seg_col, carry)


def normalize_kernel(gated_ref, sq_ref, gain_ref, out_ref):
    tiles = gated_ref.shape[1] // 128
    inverse = lax.rsqrt(sq_ref[...] / (tiles * 64 * 8) + EPS)
    spread = jnp.concatenate(
        [jnp.broadcast_to(inverse[0:1], (64, T)), jnp.broadcast_to(inverse[1:2], (64, T))], axis=0
    )
    for i in range(tiles):
        cut = slice(128 * i, 128 * i + 128)
        out_ref[cut, :] = ((gated_ref[:, cut] * gain_ref[:, cut]).T * spread).astype(BF16)


def normalize(gated, squares, gain):
    return pl.pallas_call(
        normalize_kernel,
        out_shape=jax.ShapeDtypeStruct(gated.shape[::-1], BF16),
        compiler_params=vmem(10),
        name="normalize",
    )(gated, squares, gain)


NONE = -1e30


def softmax_of(parts, values):
    top = parts[0]
    for part in parts[1:]:
        top = jnp.maximum(top, part)
    top = jnp.maximum(jnp.max(top, axis=0, keepdims=True), NONE)
    raised = [jnp.exp2(part - top) for part in parts]
    total = sum(raised)
    total = jnp.sum(total, axis=0, keepdims=True)
    some = total > 0.0
    safe = jnp.where(some, total, 1.0)
    share = jnp.where(some, 1.0 / safe, 0.0)
    out = sum(dot(value, (part * share).astype(BF16)) for part, value in zip(raised, values))
    return out, jnp.where(some, top + jnp.log2(safe), NONE)


def own_kernel(q_ref, k_ref, v_ref, segr_ref, segc_ref, out_ref, lse_ref):
    scale = LOG2E / math.sqrt(HD)
    mask = (segc_ref[...] == segr_ref[...]) & (
        lax.broadcasted_iota(jnp.int32, (T, T), 0) <= lanes_of((T, T))
    )
    lse_ref[...] = jnp.zeros_like(lse_ref)
    for h in range(q_ref.shape[0] // HD):
        at = slice(HD * h, HD * h + HD)
        part = jnp.where(mask, dot(k_ref[at, :], q_ref[at, :], 0, 0) * scale, -jnp.inf)
        out_ref[at, :], lse_ref[h : h + 1, :] = softmax_of([part], [v_ref[at, :]])


def attend_own(q, k, v, seg_row, seg_col):
    return pl.pallas_call(
        own_kernel,
        out_shape=(jax.ShapeDtypeStruct(q.shape, F32), jax.ShapeDtypeStruct((8, T), F32)),
        compiler_params=vmem(12),
        name="attend_own",
    )(q, k, v, seg_row, seg_col)


def next_kernel(q_ref, k_ref, v_ref, kv_ref, segc_ref, out_ref):
    width = k_ref.shape[0]
    scale = LOG2E / math.sqrt(HD)
    wanted = q_ref[width : width + 16, :].astype(F32)[0:1]
    ids = kv_ref[2 * width : 2 * width + 16, :].astype(F32)[0:8]
    before = jnp.concatenate([ids] * 16, axis=0).T[:, 0:1]
    masks = (segc_ref[...].astype(F32) + 1.0 == wanted, before == wanted)
    rows = []
    for h in range(width // HD):
        at = slice(HD * h, HD * h + HD)
        theirs = slice(width + HD * h, width + HD * h + HD)
        keys, values = (k_ref[at, :], kv_ref[at, :]), (v_ref[at, :], kv_ref[theirs, :])
        parts = [
            jnp.where(mask, dot(key, q_ref[at, :], 0, 0) * scale, -jnp.inf)
            for mask, key in zip(masks, keys)
        ]
        out, lse = softmax_of(parts, values)
        out_ref[at, :] = out.astype(BF16)
        for _ in range(3):
            rows.append(lse.astype(BF16).astype(F32))
            lse = lse - rows[-1]
    rows.append(jnp.ones((16 - len(rows), T), F32))
    out_ref[width : width + 16, :] = jnp.concatenate(rows, axis=0).astype(BF16)


def attend_next(q, k, v, kv, seg_col):
    return pl.pallas_call(
        next_kernel,
        out_shape=jax.ShapeDtypeStruct(q.shape, BF16),
        compiler_params=vmem(14),
        name="attend_next",
    )(q, k, v, kv, seg_col)


def merge_kernel(out_ref, lse_ref, far_ref, rows_ref):
    width = out_ref.shape[0]
    stats = far_ref[width : width + 16, :].astype(F32)
    given = stats[15:16] > 0.0
    merged = []
    for h in range(width // HD):
        at = slice(HD * h, HD * h + HD)
        lse = stats[3 * h : 3 * h + 1] + stats[3 * h + 1 : 3 * h + 2] + stats[3 * h + 2 : 3 * h + 3]
        lse = jnp.where(given, lse, NONE)
        own = lse_ref[h : h + 1, :]
        top = jnp.maximum(lse, own)
        near, far = jnp.exp2(own - top), jnp.exp2(lse - top)
        total = near + far
        merged.append(
            out_ref[at, :] * (near / total) + far_ref[at, :].astype(F32) * (far / total)
        )
    rows_ref[...] = jnp.concatenate(merged, axis=0).astype(BF16)


def merge(out, lse, far):
    return pl.pallas_call(
        merge_kernel,
        out_shape=jax.ShapeDtypeStruct(out.shape, BF16),
        compiler_params=vmem(8),
        name="merge",
    )(out, lse, far)


ORDER = (2, 1, 3, 0)


def send_out(step, refs, own_s, other_s, sems):
    for k in range(len(ORDER)):
        pair = (
            pltpu.make_async_copy(own_s.at[k], refs[2 * k], sems.at[0, k]),
            pltpu.make_async_copy(other_s.at[k], refs[2 * k + 1], sems.at[1, k]),
        )

        @pl.when(step == k)
        def _(pair=pair):
            for copy in pair:
                copy.start()

    @pl.when(step == len(ORDER) - 1)
    def _():
        for k in range(len(ORDER)):
            pltpu.make_async_copy(own_s.at[k], refs[2 * k], sems.at[0, k]).wait()
            pltpu.make_async_copy(other_s.at[k], refs[2 * k + 1], sems.at[1, k]).wait()


def block_outputs(rows):
    count = len(ORDER)
    raw = pl.BlockSpec(memory_space=pl.ANY)
    pair = [jax.ShapeDtypeStruct((rows, T), F32), jax.ShapeDtypeStruct((rows, T), BF16)]
    scratch = [
        pltpu.VMEM((count, rows, T), F32),
        pltpu.VMEM((count, rows, T), BF16),
        pltpu.SemaphoreType.DMA((2, count)),
    ]
    return pair * count, [raw] * (2 * count), scratch


def project_kernel(place_ref, att_ref, mam_ref, wa_ref, wm_ref, *refs):
    outs, (own_s, other_s, sems) = refs[:-3], refs[-3:]
    step = pl.program_id(0)
    half = own_s.shape[1]
    out = dot(wa_ref[...], att_ref[...], 0, 0) + dot(wm_ref[...], mam_ref[...], 0, 0)
    first = place_ref[len(ORDER)] == 0
    own_s[step] = jnp.where(first, out[0:half], out[half:])
    other_s[step] = jnp.where(first, out[half:], out[0:half]).astype(BF16)
    send_out(step, outs, own_s, other_s, sems)


def project(place, att, mam, wa, wm):
    rows = wa.shape[0]
    once = pl.Buffered(1)
    shapes, specs, scratch = block_outputs(rows)
    return pl.pallas_call(
        project_kernel,
        grid_spec=pltpu.PrefetchScalarGridSpec(
            num_scalar_prefetch=1,
            grid=(len(ORDER),),
            in_specs=[
                pl.BlockSpec(att.shape, lambda s, p: (0, 0), pipeline_mode=once),
                pl.BlockSpec(mam.shape, lambda s, p: (0, 0), pipeline_mode=once),
                pl.BlockSpec((rows, 2 * rows), lambda s, p: (0, p[s])),
                pl.BlockSpec((wm.shape[0], 2 * rows), lambda s, p: (0, p[s])),
            ],
            out_specs=specs,
            scratch_shapes=scratch,
        ),
        out_shape=shapes,
        compiler_params=vmem(20),
        name="project",
    )(place, att, mam, wa, wm)


def prepare_kernel(place_ref, *refs):
    z_refs, unscale_ref, rows_ref, inv_ref = refs[:-3], refs[-3], refs[-2], refs[-1]
    chips, pair = unscale_ref.shape
    mine = [ref[...] for ref in z_refs[0::2]]
    theirs = [ref[...] for ref in z_refs[1::2]]
    mine, theirs = (
        [b[0], b[1], jnp.concatenate([b[2], b[3]], axis=0), b[4]] for b in (mine, theirs)
    )
    first = place_ref[1] == 0
    total = jnp.zeros((T, 128), F32)
    for d in range(chips):
        both = jnp.concatenate(
            [jnp.where(first, mine[d], theirs[d]), jnp.where(first, theirs[d], mine[d])], axis=0
        ).T
        chip = lax.rem(place_ref[0] + chips - d, chips)
        rows_ref[:, pl.ds(pl.multiple_of(chip * pair, 128), pair)] = both
        plain = both.astype(F32) * unscale_ref[pl.ds(chip, 1), :]
        square = plain * plain
        for i in range(pair // 128):
            total = total + square[:, 128 * i : 128 * i + 128]
    inv_ref[...] = jnp.broadcast_to(
        lax.rsqrt(jnp.sum(total, axis=1, keepdims=True) / (chips * pair) + EPS), (T, 128)
    )


def prepare(place, blocks, unscale):
    smem = pl.BlockSpec(memory_space=pltpu.SMEM)
    full = pl.BlockSpec(memory_space=pltpu.VMEM)
    return pl.pallas_call(
        prepare_kernel,
        in_specs=[smem] + [full] * (len(blocks) + 1),
        out_shape=(
            jax.ShapeDtypeStruct((T, unscale.size), BF16), jax.ShapeDtypeStruct((T, 128), F32)
        ),
        compiler_params=vmem(14),
        name="prepare",
    )(place, *blocks, unscale)


def mlp_kernel(place_ref, rows_ref, inv_ref, gu_ref, down_ref, *refs):
    outs, (act_s, own_s, other_s, sems) = refs[:-4], refs[-4:]
    half, hidden = own_s.shape[1], act_s.shape[1]
    first = hidden // 128
    step = pl.program_id(0)

    @pl.when(step < first)
    def _():
        width = rows_ref.shape[1]
        w = jnp.concatenate(
            [gu_ref[:, 0].reshape(width, 128), gu_ref[:, 1].reshape(width, 128)], axis=1
        )
        both = dot(rows_ref[...], w)
        gate = both[:, 0:128] * inv_ref[...]
        up = both[:, 128:256] * inv_ref[...]
        act_s[:, pl.ds(pl.multiple_of(step * 128, 128), 128)] = (
            gate / (1.0 + jnp.exp(-gate)) * up
        ).astype(BF16)

    @pl.when(step >= first)
    def _():
        k = step - first
        out = dot(down_ref[:, 0].reshape(2 * half, hidden), act_s[...], 1, 1)
        lower = place_ref[len(ORDER)] == 0
        own_s[k] = jnp.where(lower, out[0:half], out[half:])
        other_s[k] = jnp.where(lower, out[half:], out[0:half]).astype(BF16)

    send_out(step - first, outs, own_s, other_s, sems)


def mlp(place, rows, inv, weights):
    parts, _, height, hidden = weights.shape
    once = pl.Buffered(1)
    first = hidden // 128
    count = len(ORDER)
    per = parts // count
    shapes, specs, scratch = block_outputs(per * height // 2)
    return pl.pallas_call(
        mlp_kernel,
        grid_spec=pltpu.PrefetchScalarGridSpec(
            num_scalar_prefetch=1,
            grid=(first + count,),
            in_specs=[
                pl.BlockSpec(rows.shape, lambda s, p: (0, 0), pipeline_mode=once),
                pl.BlockSpec(inv.shape, lambda s, p: (0, 0), pipeline_mode=once),
                pl.BlockSpec(
                    (parts, 2, height, 128), lambda s, p: (0, 0, 0, jnp.minimum(s, first - 1))
                ),
                pl.BlockSpec(
                    (per, 1, height, hidden), lambda s, p: (p[jnp.maximum(s - first, 0)], 2, 0, 0)
                ),
            ],
            out_specs=specs,
            scratch_shapes=[pltpu.VMEM((T, hidden), BF16), *scratch],
        ),
        out_shape=shapes,
        compiler_params=vmem(26),
        name="mlp",
    )(place, rows, inv, weights, weights)


def pages_kernel(table_ref, k_ref, v_ref, out_ref):
    pages = out_ref.shape[2]
    row = lax.broadcasted_iota(jnp.int32, (T, T), 0)
    chosen = (table_ref[...] == lax.rem(row, pages)) & (
        lax.rem(lanes_of((T, T)), PAGE) == row // pages
    )
    chosen = jnp.where(chosen, 1.0, 0.0).astype(BF16)
    for i, ref in enumerate((k_ref, v_ref)):
        for h in range(ref.shape[0] // HD):
            tokens = dot(chosen, ref[HD * h : HD * h + HD, :], 1, 1).astype(BF16)
            for j in range(PAGE):
                out_ref[i, h, :, HD * j : HD * j + HD] = tokens[pages * j : pages * j + pages]


def cache_pages(table, k, v):
    heads, pages = k.shape[0] // HD, table.shape[1]
    return pl.pallas_call(
        pages_kernel,
        out_shape=jax.ShapeDtypeStruct((2, heads, pages, PAGE * HD), BF16),
        compiler_params=vmem(10),
        name="cache_pages",
    )(jnp.repeat(table, PAGE, axis=1), k, v)


def stack_kernel(a_ref, b_ref, c_ref, out_ref, held_ref, sems):
    refs = (a_ref, b_ref, c_ref)
    loads = [pltpu.make_async_copy(r, held_ref.at[i], sems.at[0, i]) for i, r in enumerate(refs)]
    saves = [
        pltpu.make_async_copy(held_ref.at[i], out_ref.at[i], sems.at[1, i]) for i in range(len(refs))
    ]
    for load in loads:
        load.start()
    for load, save in zip(loads, saves):
        load.wait()
        save.start()
    for save in saves:
        save.wait()


def stack_three(a, b, c):
    raw = pl.BlockSpec(memory_space=pl.ANY)
    return pl.pallas_call(
        stack_kernel,
        in_specs=[raw, raw, raw],
        out_specs=raw,
        out_shape=jax.ShapeDtypeStruct((3, *a.shape), a.dtype),
        scratch_shapes=[pltpu.VMEM((3, *a.shape), a.dtype), pltpu.SemaphoreType.DMA((2, 3))],
        compiler_params=vmem(4),
        name="stack_three",
    )(in_hbm(a), in_hbm(b), in_hbm(c))


def behind(value, steps):
    count = lax.axis_size(REQ)
    pairs = [(i, i + steps) for i in range(count) if 0 <= i + steps < count]
    return lax.ppermute(value, REQ, pairs)


def along(value, steps):
    count = lax.axis_size("x")
    return lax.ppermute(value, "x", [(i, (i + steps) % count) for i in range(count)])


def swap(value):
    return lax.ppermute(value, "c", [(0, 1), (1, 0)])


def half_kernel(own_ref, other_ref, *refs, top):
    out_ref = refs[-1]
    half = out_ref.shape[0]
    at = slice(0, half) if top else slice(half, 2 * half)
    total = own_ref[at, :] + other_ref[at, :].astype(F32)
    if len(refs) == 2:
        total = total + refs[0][...].astype(F32)
    out_ref[...] = total.astype(BF16)


def add_half(own, other, *extra, top):
    return pl.pallas_call(
        functools.partial(half_kernel, top=top),
        out_shape=jax.ShapeDtypeStruct((own.shape[0] // 2, own.shape[1]), BF16),
        compiler_params=vmem(6),
        name="add_half",
    )(own, other, *extra)


def base_kernel(base_ref, own_ref, other_ref, top_ref, low_ref, out_ref):
    half = top_ref.shape[0]
    total = base_ref[...].astype(F32) + own_ref[...] + other_ref[...].astype(F32)
    out_ref[0:half, :] = total[0:half] + top_ref[...].astype(F32)
    out_ref[half:, :] = total[half:] + low_ref[...].astype(F32)


def add_base(base, own, other, top, low):
    return pl.pallas_call(
        base_kernel,
        out_shape=jax.ShapeDtypeStruct(own.shape, F32),
        compiler_params=vmem(8),
        name="add_base",
    )(base, own, other, top, low)


def mixed_kernel(base_ref, top_ref, low_ref, gain_ref, mixed_ref, scaled_ref):
    half = top_ref.shape[0]
    for at, ref in ((slice(0, half), top_ref), (slice(half, 2 * half), low_ref)):
        mixed = base_ref[at, :] + ref[...].astype(F32)
        mixed_ref[at, :] = mixed
        scaled_ref[at, :] = (mixed * gain_ref[at, :]).astype(BF16)


def finish_mixed(base, top, low, gain):
    return pl.pallas_call(
        mixed_kernel,
        out_shape=(
            jax.ShapeDtypeStruct(base.shape, F32), jax.ShapeDtypeStruct(base.shape, BF16)
        ),
        compiler_params=vmem(8),
        name="finish_mixed",
    )(base, top, low, gain)


def hidden_kernel(base_ref, top_ref, low_ref, new_ref, kept_ref, sq_ref):
    half = top_ref.shape[0]
    total = jnp.zeros(sq_ref.shape, F32)
    for at, ref in ((slice(0, half), top_ref), (slice(half, 2 * half), low_ref)):
        new = (base_ref[at, :] + ref[...].astype(F32)).astype(BF16)
        new_ref[at, :] = new
        kept_ref[at, :] = new
        wide = new.astype(F32)
        total = total + jnp.sum(wide * wide, axis=0, keepdims=True)
    sq_ref[...] = total


def finish_hidden(base, top, low):
    return pl.pallas_call(
        hidden_kernel,
        out_shape=(
            jax.ShapeDtypeStruct(base.shape, BF16), jax.ShapeDtypeStruct(base.shape, BF16),
            jax.ShapeDtypeStruct((1, T), F32),
        ),
        compiler_params=vmem(8),
        name="finish_hidden",
    )(base, top, low)


def halves_kernel(own_ref, other_ref, first_ref, second_ref):
    half = first_ref.shape[0]
    total = (own_ref[...] + other_ref[...].astype(F32)).astype(BF16)
    first_ref[...] = total[0:half]
    second_ref[...] = total[half:]


def add_halves(own, other):
    half = jax.ShapeDtypeStruct((own.shape[0] // 2, own.shape[1]), BF16)
    return pl.pallas_call(
        halves_kernel, out_shape=(half, half), compiler_params=vmem(6), name="add_halves"
    )(own, other)


def scatter_sum(blocks, base):
    own2, other2, own1, other1, own3, other3, own0, other0 = blocks
    up, low = add_halves(own2, swap(other2))
    up, low = along(up, 1), along(low, 3)
    other1, other3, other0 = swap(other1), swap(other3), swap(other0)
    left_low = along(add_half(own1, other1, top=False), 1)
    right_top = along(add_half(own3, other3, top=True), 3)
    left_top = along(add_half(own1, other1, up, top=True), 1)
    right_low = along(add_half(own3, other3, low, top=False), 3)
    return add_base(base, own0, other0, right_top, left_low), left_top, right_low


def gather_rows(share):
    half = share.shape[0] // 2
    left, right = along(share, 1), along(share, 3)
    first, second = along(left[:half], 1), along(right[half:], 3)
    got = []
    for block in (share, left, first, second, right):
        got += [block, swap(block)]
    return got


def group_sum(value):
    paired = value + swap(value)
    return paired + along(paired, 1) + along(paired, 2) + along(paired, 3)


def body(
    hidden, query_heads, key_heads, value_heads, segment_ids, page_table, mamba_conv_input,
    mamba_output_gate, state_input_projection, state_output_projection, discrete_step_size,
    head_decay_rate, skip_gain, mamba_gated_norm_gain, attn_proj, mamba_output_projection,
    mlp_norm_gain, gate_proj, up_proj, down_proj, next_norm_gain,
):
    row_count = query_heads.shape[0]
    width = hidden.shape[1]
    total_width = mlp_norm_gain.shape[0]
    owner = lax.axis_index("x") * lax.axis_size("c") + lax.axis_index("c")

    x = lax.axis_index("x")
    core = lax.axis_index("c")

    place = jnp.stack([(x + steps) % 4 for steps in ORDER] + [core]).astype(jnp.int32)

    stacked_weights = stack_three(gate_proj, up_proj, down_proj.T)
    weights = in_hbm(lax.all_gather(stacked_weights, REQ, axis=0, tiled=False))

    seg_row = segment_ids.reshape(1, row_count)
    seg_col = segment_ids.reshape(row_count, 1)
    state, row, col = leaving_state(
        discrete_step_size.T, head_decay_rate.reshape(-1, 1), seg_row, mamba_conv_input,
        state_input_projection,
    )
    near = behind(state, 1)

    q, k, v = query_heads.T, key_heads.T, value_heads.T
    ids = jnp.broadcast_to((segment_ids + 1).astype(BF16)[None, :], (16, row_count))
    kv1 = behind(jnp.concatenate([k, v, ids], axis=0), 1)
    next_q = behind(jnp.concatenate([q, ids], axis=0), -1)

    kv_cache = cache_pages(page_table, k, v)
    own_out, own_lse = attend_own(q, k, v, seg_row, seg_col)
    skip = jnp.repeat(skip_gain, mamba_conv_input.shape[1] // skip_gain.shape[0]).reshape(1, -1)
    local = mamba_local(
        mamba_conv_input, state_input_projection, state_output_projection, row, col, seg_row,
        seg_col, skip,
    )
    waited_col, own_lse, local, kv_cache = lax.optimization_barrier(
        (seg_col, own_lse, local, kv_cache)
    )
    next_out = attend_next(next_q, k, v, kv1, waited_col)
    far_out = behind(next_out, 1)
    state, near, _ = lax.optimization_barrier((state, near, next_out))
    carry = behind(pass_through(state, near), 1)
    gated, squares = mamba_finish(
        in_hbm(local), mamba_output_gate, state_output_projection, col, seg_col, carry
    )
    mam = normalize(gated, group_sum(squares), mamba_gated_norm_gain.reshape(1, -1))
    own_out, mam = lax.optimization_barrier((own_out, mam))
    att = merge(in_hbm(own_out), own_lse, far_out)
    attn_proj, mamba_output_projection = in_hbm(attn_proj), in_hbm(mamba_output_projection)
    own_gain = lax.dynamic_slice_in_dim(mlp_norm_gain, owner * width, width, 0)
    mixed, scaled = finish_mixed(
        *scatter_sum(project(place, att, mam, attn_proj, mamba_output_projection), hidden.T),
        own_gain[:, None],
    )
    blocks = gather_rows(scaled)
    here = jnp.stack([x, core]).astype(jnp.int32)
    rows, inv = prepare(here, blocks, (1.0 / mlp_norm_gain).reshape(4, -1))
    new_hidden, kept, squares = finish_hidden(
        *scatter_sum(mlp(place, in_hbm(rows), inv, weights), mixed)
    )
    widened = kept.astype(F32)
    total_sq = group_sum(squares)
    next_normed = (
        widened * lax.rsqrt(total_sq / total_width + EPS) * next_norm_gain[:, None]
    ).astype(BF16)

    return (new_hidden.T, next_normed.T, kv_cache)


def solution(mesh):
    split = Mesh(mesh.devices.reshape(4, 4, 4, 2), ("z", "y", "x", "c"))
    tokens = P(REQ, MLP)
    return jax.shard_map(
        body,
        mesh=split,
        in_specs=(
            tokens, tokens, tokens, tokens, P(REQ), P(REQ, None), tokens, tokens, P(REQ, None),
            P(REQ, None), tokens, P(MLP), P(MLP), P(MLP), P(MLP, None), P(MLP, None), P(), tokens,
            tokens, P(MLP, REQ), P(MLP),
        ),
        out_specs=(tokens, tokens, P(None, MLP, REQ, None)),
        check_vma=False,
    )
```

```python
import functools
import math

import jax
import jax.numpy as jnp
from jax import lax
from jax.experimental import pallas as pl
from jax.experimental.pallas import tpu as pltpu
from jax.sharding import Mesh
from jax.sharding import PartitionSpec as P

HD = 224
PAGE = 16
EPS = 1e-05
LOG2E = math.log2(math.e)
T = 512
F32 = jnp.float32
BF16 = jnp.bfloat16
REQ = ("z", "y")
MLP = ("x", "c")


def vmem(mib):
    return pltpu.CompilerParams(vmem_limit_bytes=mib << 20)


def in_hbm(value):
    return pltpu.with_memory_space_constraint(value, pltpu.HBM)


def dot(a, b, ca=1, cb=0):
    return lax.dot_general(a, b, (((ca,), (cb,)), ((), ())), preferred_element_type=F32)


def lanes_of(shape):
    return lax.broadcasted_iota(jnp.int32, shape, 1)


def halves(pair, i, rows, base=0):
    low = jnp.broadcast_to(pair[:, base + 2 * i : base + 2 * i + 1], (rows, 128))
    high = jnp.broadcast_to(pair[:, base + 2 * i + 1 : base + 2 * i + 2], (rows, 128))
    return jnp.where(lanes_of((rows, 128)) < 64, low, high)


def state_kernel(dt_ref, rate_ref, seg_ref, x_ref, b_ref, state_ref, row_ref, col_ref, tmp_ref):
    heads = dt_ref.shape[0]
    tiles = x_ref.shape[1] // 128
    tmp_ref[...] = jnp.zeros_like(tmp_ref)
    tmp_ref[0:heads, :] = dt_ref[...] * (rate_ref[...] * -LOG2E)
    tmp_ref[16:32, :] = jnp.ones((16, T), F32)
    tmp_ref[16 : 16 + heads, :] = dt_ref[...]
    run = tmp_ref[0:16, :]
    lane = lanes_of((16, T))
    shift = 1
    while shift < T:
        run = run + jnp.where(lane >= shift, pltpu.roll(run, shift, 1), 0.0)
        shift *= 2
    row = run - jnp.log2(tmp_ref[16:32, :])
    row_ref[...] = row
    last = jnp.sum(jnp.where(lane == T - 1, run, 0.0), axis=1, keepdims=True)
    seg = seg_ref[...]
    tail = jnp.where(seg == jnp.max(seg), 1.0, 0.0)
    tmp_ref[0:16, :] = run
    tmp_ref[16:32, :] = jnp.exp2(last - row) * tail
    col = tmp_ref[...].T
    col_ref[...] = col
    b_rows = b_ref[...].astype(F32).T.astype(BF16)
    for i in range(tiles):
        cut = slice(128 * i, 128 * i + 128)
        weighted = (x_ref[:, cut].astype(F32) * halves(col, i, T, 16)).astype(BF16)
        both = dot(b_rows, weighted)
        kept = jnp.where(lanes_of((64, 128)) < 64, both[0:64], both[64:128])
        state_ref[0:64, cut] = kept.astype(BF16)
        gone = jnp.exp2(halves(col[T - 8 : T], i, 8))[7:8]
        final = jnp.broadcast_to((jnp.max(seg) + 1).astype(F32), (8, 128))
        state_ref[64:80, cut] = jnp.concatenate(
            [jnp.broadcast_to(gone, (8, 128)), final], axis=0
        ).astype(BF16)


def leaving_state(dt_rows, rate, seg_row, x, b):
    width = x.shape[1]
    return pl.pallas_call(
        state_kernel,
        out_shape=(
            jax.ShapeDtypeStruct((80, width), BF16),
            jax.ShapeDtypeStruct((16, T), F32),
            jax.ShapeDtypeStruct((T, 128), F32),
        ),
        scratch_shapes=[pltpu.VMEM((128, T), F32)],
        compiler_params=vmem(12),
        name="leaving_state",
    )(dt_rows, rate, seg_row, x, b)


def through_kernel(state_ref, near_ref, out_ref):
    tail = state_ref[64:80, :].astype(F32)
    before = near_ref[64:80, :].astype(F32)
    passes = jnp.where(tail[8:9] == before[8:9], tail[0:1], 0.0)
    out_ref[0:64, :] = (
        state_ref[0:64, :].astype(F32) + passes * near_ref[0:64, :].astype(F32)
    ).astype(BF16)
    out_ref[64:80, :] = state_ref[64:80, :]


def pass_through(state, near):
    return pl.pallas_call(
        through_kernel,
        out_shape=jax.ShapeDtypeStruct(state.shape, BF16),
        compiler_params=vmem(4),
        name="pass_through",
    )(state, near)


HALF = T // 2


def local_kernel(x_ref, b_ref, c_ref, row_ref, col_ref, segr_ref, segc_ref, skip_ref, out_ref, inner_ref):
    tiles = x_ref.shape[1] // 128
    b = b_ref[...]
    c = c_ref[...]
    live = (segc_ref[...] == segr_ref[...]) & (
        lax.broadcasted_iota(jnp.int32, (T, T), 0) >= lanes_of((T, T))
    )
    group = lanes_of((T, 128)) < 64
    for g in range(2):
        own = jnp.where(group == (g == 0), c, jnp.zeros_like(c))
        inner_ref[g] = jnp.where(live, dot(own, b, 1, 1), 0.0)
    col = col_ref[...]
    lane = lanes_of((T, 128))
    low = lanes_of((HALF, 128)) < 64

    def tile(i, _):
        cut = pl.ds(pl.multiple_of(i * 128, 128), 128)
        decays = [
            jnp.sum(jnp.where(lane == 2 * i + g, col, 0.0), axis=1, keepdims=True) for g in range(2)
        ]
        rows_of = [row_ref[pl.ds(2 * i + g, 1), :] for g in range(2)]
        for k in range(2):
            rows = slice(HALF * k, HALF * k + HALF)
            upto = HALF * (k + 1)
            parts = []
            for g in range(2):
                power = jnp.minimum(decays[g][rows] - rows_of[g][:, 0:upto], 126.0)
                mixing = (jnp.exp2(power) * inner_ref[g, rows, 0:upto]).astype(BF16)
                parts.append(dot(mixing, x_ref[0:upto, cut]))
            y = jnp.where(low, parts[0], parts[1])
            out_ref[rows, cut] = y + skip_ref[:, cut] * x_ref[rows, cut].astype(F32)
        return 0

    lax.fori_loop(0, tiles, tile, 0)


def mamba_local(x, b, c, row, col, seg_row, seg_col, skip):
    return pl.pallas_call(
        local_kernel,
        out_shape=jax.ShapeDtypeStruct(x.shape, F32),
        scratch_shapes=[pltpu.VMEM((2, T, T), F32)],
        compiler_params=vmem(14),
        name="mamba_local",
    )(x, b, c, row, col, seg_row, seg_col, skip)


def finish_kernel(y_ref, z_ref, c_ref, col_ref, segc_ref, carry_ref, out_ref, sq_ref):
    tiles = y_ref.shape[1] // 128
    c = c_ref[...]
    last = jnp.max(carry_ref[64:80, 0:128].astype(F32)[8:16])
    enters = segc_ref[...].astype(F32) + 1.0 == last
    entry = jnp.where(enters, jnp.exp2(col_ref[...]), 0.0)
    first = lanes_of((64, 128)) < 64
    total = jnp.zeros((T, 128), F32)
    for i in range(tiles):
        cut = slice(128 * i, 128 * i + 128)
        carry = carry_ref[0:64, cut]
        nothing = jnp.zeros_like(carry)
        spread_state = jnp.concatenate(
            [jnp.where(first, carry, nothing), jnp.where(first, nothing, carry)], axis=0
        )
        y = y_ref[:, cut] + halves(entry, i, T) * dot(c, spread_state)
        z = z_ref[:, cut].astype(F32)
        gated = y * (z / (1.0 + jnp.exp(-z)))
        out_ref[:, cut] = gated
        total = total + gated * gated
    turned = total.T
    even = jnp.sum(turned[0:64], axis=0, keepdims=True)
    odd = jnp.sum(turned[64:128], axis=0, keepdims=True)
    sq_ref[...] = jnp.concatenate([even, odd], axis=0)


def mamba_finish(y, z, c, col, seg_col, carry):
    return pl.pallas_call(
        finish_kernel,
        out_shape=(jax.ShapeDtypeStruct(y.shape, F32), jax.ShapeDtypeStruct((2, T), F32)),
        compiler_params=vmem(14),
        name="mamba_finish",
    )(y, z, c, col, seg_col, carry)


def normalize_kernel(gated_ref, sq_ref, gain_ref, out_ref):
    tiles = gated_ref.shape[1] // 128
    inverse = lax.rsqrt(sq_ref[...] / (tiles * 64 * 8) + EPS)
    spread = jnp.concatenate(
        [jnp.broadcast_to(inverse[0:1], (64, T)), jnp.broadcast_to(inverse[1:2], (64, T))], axis=0
    )
    for i in range(tiles):
        cut = slice(128 * i, 128 * i + 128)
        out_ref[cut, :] = ((gated_ref[:, cut] * gain_ref[:, cut]).T * spread).astype(BF16)


def normalize(gated, squares, gain):
    return pl.pallas_call(
        normalize_kernel,
        out_shape=jax.ShapeDtypeStruct(gated.shape[::-1], BF16),
        compiler_params=vmem(10),
        name="normalize",
    )(gated, squares, gain)


NONE = -1e30


def softmax_of(parts, values):
    top = parts[0]
    for part in parts[1:]:
        top = jnp.maximum(top, part)
    top = jnp.maximum(jnp.max(top, axis=0, keepdims=True), NONE)
    raised = [jnp.exp2(part - top) for part in parts]
    total = sum(raised)
    total = jnp.sum(total, axis=0, keepdims=True)
    some = total > 0.0
    safe = jnp.where(some, total, 1.0)
    share = jnp.where(some, 1.0 / safe, 0.0)
    out = sum(dot(value, (part * share).astype(BF16)) for part, value in zip(raised, values))
    return out, jnp.where(some, top + jnp.log2(safe), NONE)


def own_kernel(q_ref, k_ref, v_ref, segr_ref, segc_ref, out_ref, lse_ref):
    scale = LOG2E / math.sqrt(HD)
    mask = (segc_ref[...] == segr_ref[...]) & (
        lax.broadcasted_iota(jnp.int32, (T, T), 0) <= lanes_of((T, T))
    )
    lse_ref[...] = jnp.zeros_like(lse_ref)
    for h in range(q_ref.shape[0] // HD):
        at = slice(HD * h, HD * h + HD)
        part = jnp.where(mask, dot(k_ref[at, :], q_ref[at, :], 0, 0) * scale, -jnp.inf)
        out_ref[at, :], lse_ref[h : h + 1, :] = softmax_of([part], [v_ref[at, :]])


def attend_own(q, k, v, seg_row, seg_col):
    return pl.pallas_call(
        own_kernel,
        out_shape=(jax.ShapeDtypeStruct(q.shape, F32), jax.ShapeDtypeStruct((8, T), F32)),
        compiler_params=vmem(12),
        name="attend_own",
    )(q, k, v, seg_row, seg_col)


def next_kernel(q_ref, k_ref, v_ref, kv_ref, segc_ref, out_ref):
    width = k_ref.shape[0]
    scale = LOG2E / math.sqrt(HD)
    wanted = q_ref[width : width + 16, :].astype(F32)[0:1]
    ids = kv_ref[2 * width : 2 * width + 16, :].astype(F32)[0:8]
    before = jnp.concatenate([ids] * 16, axis=0).T[:, 0:1]
    masks = (segc_ref[...].astype(F32) + 1.0 == wanted, before == wanted)
    rows = []
    for h in range(width // HD):
        at = slice(HD * h, HD * h + HD)
        theirs = slice(width + HD * h, width + HD * h + HD)
        keys, values = (k_ref[at, :], kv_ref[at, :]), (v_ref[at, :], kv_ref[theirs, :])
        parts = [
            jnp.where(mask, dot(key, q_ref[at, :], 0, 0) * scale, -jnp.inf)
            for mask, key in zip(masks, keys)
        ]
        out, lse = softmax_of(parts, values)
        out_ref[at, :] = out.astype(BF16)
        for _ in range(3):
            rows.append(lse.astype(BF16).astype(F32))
            lse = lse - rows[-1]
    rows.append(jnp.ones((16 - len(rows), T), F32))
    out_ref[width : width + 16, :] = jnp.concatenate(rows, axis=0).astype(BF16)


def attend_next(q, k, v, kv, seg_col):
    return pl.pallas_call(
        next_kernel,
        out_shape=jax.ShapeDtypeStruct(q.shape, BF16),
        compiler_params=vmem(14),
        name="attend_next",
    )(q, k, v, kv, seg_col)


def merge_kernel(out_ref, lse_ref, far_ref, rows_ref):
    width = out_ref.shape[0]
    stats = far_ref[width : width + 16, :].astype(F32)
    given = stats[15:16] > 0.0
    merged = []
    for h in range(width // HD):
        at = slice(HD * h, HD * h + HD)
        lse = stats[3 * h : 3 * h + 1] + stats[3 * h + 1 : 3 * h + 2] + stats[3 * h + 2 : 3 * h + 3]
        lse = jnp.where(given, lse, NONE)
        own = lse_ref[h : h + 1, :]
        top = jnp.maximum(lse, own)
        near, far = jnp.exp2(own - top), jnp.exp2(lse - top)
        total = near + far
        merged.append(
            out_ref[at, :] * (near / total) + far_ref[at, :].astype(F32) * (far / total)
        )
    rows_ref[...] = jnp.concatenate(merged, axis=0).astype(BF16)


def merge(out, lse, far):
    return pl.pallas_call(
        merge_kernel,
        out_shape=jax.ShapeDtypeStruct(out.shape, BF16),
        compiler_params=vmem(8),
        name="merge",
    )(out, lse, far)


ORDER = (2, 1, 3, 0)


def send_out(step, refs, own_s, other_s, sems):
    for k in range(len(ORDER)):
        pair = (
            pltpu.make_async_copy(own_s.at[k], refs[2 * k], sems.at[0, k]),
            pltpu.make_async_copy(other_s.at[k], refs[2 * k + 1], sems.at[1, k]),
        )

        @pl.when(step == k)
        def _(pair=pair):
            for copy in pair:
                copy.start()

    @pl.when(step == len(ORDER) - 1)
    def _():
        for k in range(len(ORDER)):
            pltpu.make_async_copy(own_s.at[k], refs[2 * k], sems.at[0, k]).wait()
            pltpu.make_async_copy(other_s.at[k], refs[2 * k + 1], sems.at[1, k]).wait()


def block_outputs(rows):
    count = len(ORDER)
    raw = pl.BlockSpec(memory_space=pl.ANY)
    pair = [jax.ShapeDtypeStruct((rows, T), F32), jax.ShapeDtypeStruct((rows, T), BF16)]
    scratch = [
        pltpu.VMEM((count, rows, T), F32),
        pltpu.VMEM((count, rows, T), BF16),
        pltpu.SemaphoreType.DMA((2, count)),
    ]
    return pair * count, [raw] * (2 * count), scratch


def project_kernel(place_ref, att_ref, mam_ref, wa_ref, wm_ref, *refs):
    outs, (own_s, other_s, sems) = refs[:-3], refs[-3:]
    step = pl.program_id(0)
    half = own_s.shape[1]
    out = dot(wa_ref[...], att_ref[...], 0, 0) + dot(wm_ref[...], mam_ref[...], 0, 0)
    first = place_ref[len(ORDER)] == 0
    own_s[step] = jnp.where(first, out[0:half], out[half:])
    other_s[step] = jnp.where(first, out[half:], out[0:half]).astype(BF16)
    send_out(step, outs, own_s, other_s, sems)


def project(place, att, mam, wa, wm):
    rows = wa.shape[0]
    once = pl.Buffered(1)
    shapes, specs, scratch = block_outputs(rows)
    return pl.pallas_call(
        project_kernel,
        grid_spec=pltpu.PrefetchScalarGridSpec(
            num_scalar_prefetch=1,
            grid=(len(ORDER),),
            in_specs=[
                pl.BlockSpec(att.shape, lambda s, p: (0, 0), pipeline_mode=once),
                pl.BlockSpec(mam.shape, lambda s, p: (0, 0), pipeline_mode=once),
                pl.BlockSpec((rows, 2 * rows), lambda s, p: (0, p[s])),
                pl.BlockSpec((wm.shape[0], 2 * rows), lambda s, p: (0, p[s])),
            ],
            out_specs=specs,
            scratch_shapes=scratch,
        ),
        out_shape=shapes,
        compiler_params=vmem(20),
        name="project",
    )(place, att, mam, wa, wm)


def prepare_kernel(place_ref, *refs):
    z_refs, unscale_ref, rows_ref, inv_ref = refs[:-3], refs[-3], refs[-2], refs[-1]
    chips, pair = unscale_ref.shape
    mine = [ref[...] for ref in z_refs[0::2]]
    theirs = [ref[...] for ref in z_refs[1::2]]
    mine, theirs = (
        [b[0], b[1], jnp.concatenate([b[2], b[3]], axis=0), b[4]] for b in (mine, theirs)
    )
    first = place_ref[1] == 0
    total = jnp.zeros((T, 128), F32)
    for d in range(chips):
        both = jnp.concatenate(
            [jnp.where(first, mine[d], theirs[d]), jnp.where(first, theirs[d], mine[d])], axis=0
        ).T
        chip = lax.rem(place_ref[0] + chips - d, chips)
        rows_ref[:, pl.ds(pl.multiple_of(chip * pair, 128), pair)] = both
        plain = both.astype(F32) * unscale_ref[pl.ds(chip, 1), :]
        square = plain * plain
        for i in range(pair // 128):
            total = total + square[:, 128 * i : 128 * i + 128]
    inv_ref[...] = jnp.broadcast_to(
        lax.rsqrt(jnp.sum(total, axis=1, keepdims=True) / (chips * pair) + EPS), (T, 128)
    )


def prepare(place, blocks, unscale):
    smem = pl.BlockSpec(memory_space=pltpu.SMEM)
    full = pl.BlockSpec(memory_space=pltpu.VMEM)
    return pl.pallas_call(
        prepare_kernel,
        in_specs=[smem] + [full] * (len(blocks) + 1),
        out_shape=(
            jax.ShapeDtypeStruct((T, unscale.size), BF16), jax.ShapeDtypeStruct((T, 128), F32)
        ),
        compiler_params=vmem(14),
        name="prepare",
    )(place, *blocks, unscale)


def mlp_kernel(place_ref, rows_ref, inv_ref, gu_ref, down_ref, *refs):
    outs, (act_s, own_s, other_s, sems) = refs[:-4], refs[-4:]
    half, hidden = own_s.shape[1], act_s.shape[1]
    first = hidden // 128
    step = pl.program_id(0)

    @pl.when(step < first)
    def _():
        width = rows_ref.shape[1]
        w = jnp.concatenate(
            [gu_ref[:, 0].reshape(width, 128), gu_ref[:, 1].reshape(width, 128)], axis=1
        )
        both = dot(rows_ref[...], w)
        gate = both[:, 0:128] * inv_ref[...]
        up = both[:, 128:256] * inv_ref[...]
        act_s[:, pl.ds(pl.multiple_of(step * 128, 128), 128)] = (
            gate / (1.0 + jnp.exp(-gate)) * up
        ).astype(BF16)

    @pl.when(step >= first)
    def _():
        k = step - first
        out = dot(down_ref[:, 0].reshape(2 * half, hidden), act_s[...], 1, 1)
        lower = place_ref[len(ORDER)] == 0
        own_s[k] = jnp.where(lower, out[0:half], out[half:])
        other_s[k] = jnp.where(lower, out[half:], out[0:half]).astype(BF16)

    send_out(step - first, outs, own_s, other_s, sems)


def mlp(place, rows, inv, weights):
    parts, _, height, hidden = weights.shape
    once = pl.Buffered(1)
    first = hidden // 128
    count = len(ORDER)
    per = parts // count
    shapes, specs, scratch = block_outputs(per * height // 2)
    return pl.pallas_call(
        mlp_kernel,
        grid_spec=pltpu.PrefetchScalarGridSpec(
            num_scalar_prefetch=1,
            grid=(first + count,),
            in_specs=[
                pl.BlockSpec(rows.shape, lambda s, p: (0, 0), pipeline_mode=once),
                pl.BlockSpec(inv.shape, lambda s, p: (0, 0), pipeline_mode=once),
                pl.BlockSpec(
                    (parts, 2, height, 128), lambda s, p: (0, 0, 0, jnp.minimum(s, first - 1))
                ),
                pl.BlockSpec(
                    (per, 1, height, hidden), lambda s, p: (p[jnp.maximum(s - first, 0)], 2, 0, 0)
                ),
            ],
            out_specs=specs,
            scratch_shapes=[pltpu.VMEM((T, hidden), BF16), *scratch],
        ),
        out_shape=shapes,
        compiler_params=vmem(26),
        name="mlp",
    )(place, rows, inv, weights, weights)


def copy_kernel(in_ref, out_ref):
    out_ref[...] = in_ref[...]


def copy_out(value):
    return pl.pallas_call(
        copy_kernel,
        out_shape=jax.ShapeDtypeStruct(value.shape, value.dtype),
        compiler_params=vmem(4),
        name="copy_out",
    )(value)


def pages_kernel(table_ref, k_ref, v_ref, out_ref):
    pages = out_ref.shape[2]
    row = lax.broadcasted_iota(jnp.int32, (T, T), 0)
    chosen = (table_ref[...] == lax.rem(row, pages)) & (
        lax.rem(lanes_of((T, T)), PAGE) == row // pages
    )
    chosen = jnp.where(chosen, 1.0, 0.0).astype(BF16)
    for i, ref in enumerate((k_ref, v_ref)):
        for h in range(ref.shape[0] // HD):
            tokens = dot(chosen, ref[HD * h : HD * h + HD, :], 1, 1).astype(BF16)
            for j in range(PAGE):
                out_ref[i, h, :, HD * j : HD * j + HD] = tokens[pages * j : pages * j + pages]


def cache_pages(table, k, v):
    heads, pages = k.shape[0] // HD, table.shape[1]
    return pl.pallas_call(
        pages_kernel,
        out_shape=jax.ShapeDtypeStruct((2, heads, pages, PAGE * HD), BF16),
        compiler_params=vmem(10),
        name="cache_pages",
    )(jnp.repeat(table, PAGE, axis=1), k, v)


def stack_kernel(a_ref, b_ref, c_ref, out_ref, held_ref, sems):
    refs = (a_ref, b_ref, c_ref)
    loads = [pltpu.make_async_copy(r, held_ref.at[i], sems.at[0, i]) for i, r in enumerate(refs)]
    saves = [
        pltpu.make_async_copy(held_ref.at[i], out_ref.at[i], sems.at[1, i]) for i in range(len(refs))
    ]
    for load in loads:
        load.start()
    for load, save in zip(loads, saves):
        load.wait()
        save.start()
    for save in saves:
        save.wait()


def stack_three(a, b, c):
    raw = pl.BlockSpec(memory_space=pl.ANY)
    return pl.pallas_call(
        stack_kernel,
        in_specs=[raw, raw, raw],
        out_specs=raw,
        out_shape=jax.ShapeDtypeStruct((3, *a.shape), a.dtype),
        scratch_shapes=[pltpu.VMEM((3, *a.shape), a.dtype), pltpu.SemaphoreType.DMA((2, 3))],
        compiler_params=vmem(4),
        name="stack_three",
    )(in_hbm(a), in_hbm(b), in_hbm(c))


def behind(value, steps):
    count = lax.axis_size(REQ)
    pairs = [(i, i + steps) for i in range(count) if 0 <= i + steps < count]
    return lax.ppermute(value, REQ, pairs)


def along(value, steps):
    count = lax.axis_size("x")
    return lax.ppermute(value, "x", [(i, (i + steps) % count) for i in range(count)])


def swap(value):
    return lax.ppermute(value, "c", [(0, 1), (1, 0)])


def half_kernel(own_ref, other_ref, *refs, top):
    out_ref = refs[-1]
    half = out_ref.shape[0]
    at = slice(0, half) if top else slice(half, 2 * half)
    total = own_ref[at, :] + other_ref[at, :].astype(F32)
    if len(refs) == 2:
        total = total + refs[0][...].astype(F32)
    out_ref[...] = total.astype(BF16)


def add_half(own, other, *extra, top):
    return pl.pallas_call(
        functools.partial(half_kernel, top=top),
        out_shape=jax.ShapeDtypeStruct((own.shape[0] // 2, own.shape[1]), BF16),
        compiler_params=vmem(6),
        name="add_half",
    )(own, other, *extra)


def base_kernel(base_ref, own_ref, other_ref, top_ref, low_ref, out_ref):
    half = top_ref.shape[0]
    total = base_ref[...].astype(F32) + own_ref[...] + other_ref[...].astype(F32)
    out_ref[0:half, :] = total[0:half] + top_ref[...].astype(F32)
    out_ref[half:, :] = total[half:] + low_ref[...].astype(F32)


def add_base(base, own, other, top, low):
    return pl.pallas_call(
        base_kernel,
        out_shape=jax.ShapeDtypeStruct(own.shape, F32),
        compiler_params=vmem(8),
        name="add_base",
    )(base, own, other, top, low)


def mixed_kernel(base_ref, top_ref, low_ref, gain_ref, mixed_ref, scaled_ref):
    half = top_ref.shape[0]
    for at, ref in ((slice(0, half), top_ref), (slice(half, 2 * half), low_ref)):
        mixed = base_ref[at, :] + ref[...].astype(F32)
        mixed_ref[at, :] = mixed
        scaled_ref[at, :] = (mixed * gain_ref[at, :]).astype(BF16)


def finish_mixed(base, top, low, gain):
    return pl.pallas_call(
        mixed_kernel,
        out_shape=(
            jax.ShapeDtypeStruct(base.shape, F32), jax.ShapeDtypeStruct(base.shape, BF16)
        ),
        compiler_params=vmem(8),
        name="finish_mixed",
    )(base, top, low, gain)


def hidden_kernel(base_ref, top_ref, low_ref, kept_ref, sq_ref):
    half = top_ref.shape[0]
    total = jnp.zeros(sq_ref.shape, F32)
    for at, ref in ((slice(0, half), top_ref), (slice(half, 2 * half), low_ref)):
        new = (base_ref[at, :] + ref[...].astype(F32)).astype(BF16)
        kept_ref[at, :] = new
        wide = new.astype(F32)
        total = total + jnp.sum(wide * wide, axis=0, keepdims=True)
    sq_ref[...] = total


def finish_hidden(base, top, low):
    return pl.pallas_call(
        hidden_kernel,
        out_shape=(
            jax.ShapeDtypeStruct(base.shape, BF16), jax.ShapeDtypeStruct((1, T), F32)
        ),
        compiler_params=vmem(8),
        name="finish_hidden",
    )(base, top, low)


def halves_kernel(own_ref, other_ref, first_ref, second_ref):
    half = first_ref.shape[0]
    total = (own_ref[...] + other_ref[...].astype(F32)).astype(BF16)
    first_ref[...] = total[0:half]
    second_ref[...] = total[half:]


def add_halves(own, other):
    half = jax.ShapeDtypeStruct((own.shape[0] // 2, own.shape[1]), BF16)
    return pl.pallas_call(
        halves_kernel, out_shape=(half, half), compiler_params=vmem(6), name="add_halves"
    )(own, other)


def scatter_sum(blocks, base):
    own2, other2, own1, other1, own3, other3, own0, other0 = blocks
    up, low = add_halves(own2, swap(other2))
    up, low = along(up, 1), along(low, 3)
    other1, other3, other0 = swap(other1), swap(other3), swap(other0)
    left_low = along(add_half(own1, other1, top=False), 1)
    right_top = along(add_half(own3, other3, top=True), 3)
    left_top = along(add_half(own1, other1, up, top=True), 1)
    right_low = along(add_half(own3, other3, low, top=False), 3)
    return add_base(base, own0, other0, right_top, left_low), left_top, right_low


def gather_rows(share):
    half = share.shape[0] // 2
    left, right = along(share, 1), along(share, 3)
    first, second = along(left[:half], 1), along(right[half:], 3)
    got = []
    for block in (share, left, first, second, right):
        got += [block, swap(block)]
    return got


def group_sum(value):
    paired = value + swap(value)
    return paired + along(paired, 1) + along(paired, 2) + along(paired, 3)


def body(
    hidden, query_heads, key_heads, value_heads, segment_ids, page_table, mamba_conv_input,
    mamba_output_gate, state_input_projection, state_output_projection, discrete_step_size,
    head_decay_rate, skip_gain, mamba_gated_norm_gain, attn_proj, mamba_output_projection,
    mlp_norm_gain, gate_proj, up_proj, down_proj, next_norm_gain,
):
    row_count = query_heads.shape[0]
    width = hidden.shape[1]
    total_width = mlp_norm_gain.shape[0]
    owner = lax.axis_index("x") * lax.axis_size("c") + lax.axis_index("c")

    x = lax.axis_index("x")
    core = lax.axis_index("c")

    place = jnp.stack([(x + steps) % 4 for steps in ORDER] + [core]).astype(jnp.int32)

    stacked_weights = stack_three(gate_proj, up_proj, down_proj.T)
    weights = in_hbm(lax.all_gather(stacked_weights, REQ, axis=0, tiled=False))

    seg_row = segment_ids.reshape(1, row_count)
    seg_col = segment_ids.reshape(row_count, 1)
    state, row, col = leaving_state(
        discrete_step_size.T, head_decay_rate.reshape(-1, 1), seg_row, mamba_conv_input,
        state_input_projection,
    )
    near = behind(state, 1)

    q, k, v = query_heads.T, key_heads.T, value_heads.T
    ids = jnp.broadcast_to((segment_ids + 1).astype(BF16)[None, :], (16, row_count))
    kv1 = behind(jnp.concatenate([k, v, ids], axis=0), 1)
    next_q = behind(jnp.concatenate([q, ids], axis=0), -1)

    kv_cache = cache_pages(page_table, k, v)
    own_out, own_lse = attend_own(q, k, v, seg_row, seg_col)
    skip = jnp.repeat(skip_gain, mamba_conv_input.shape[1] // skip_gain.shape[0]).reshape(1, -1)
    local = mamba_local(
        mamba_conv_input, state_input_projection, state_output_projection, row, col, seg_row,
        seg_col, skip,
    )
    waited_col, own_lse, local, kv_cache = lax.optimization_barrier(
        (seg_col, own_lse, local, kv_cache)
    )
    next_out = attend_next(next_q, k, v, kv1, waited_col)
    far_out = behind(next_out, 1)
    state, near, _ = lax.optimization_barrier((state, near, next_out))
    carry = behind(pass_through(state, near), 1)
    gated, squares = mamba_finish(
        in_hbm(local), mamba_output_gate, state_output_projection, col, seg_col, carry
    )
    mam = normalize(gated, group_sum(squares), mamba_gated_norm_gain.reshape(1, -1))
    own_out, mam = lax.optimization_barrier((own_out, mam))
    att = merge(in_hbm(own_out), own_lse, far_out)
    attn_proj, mamba_output_projection = in_hbm(attn_proj), in_hbm(mamba_output_projection)
    own_gain = lax.dynamic_slice_in_dim(mlp_norm_gain, owner * width, width, 0)
    mixed, scaled = finish_mixed(
        *scatter_sum(project(place, att, mam, attn_proj, mamba_output_projection), hidden.T),
        own_gain[:, None],
    )
    blocks = gather_rows(scaled)
    here = jnp.stack([x, core]).astype(jnp.int32)
    rows, inv = prepare(here, blocks, (1.0 / mlp_norm_gain).reshape(4, -1))
    kept, squares = finish_hidden(*scatter_sum(mlp(place, in_hbm(rows), inv, weights), mixed))
    new_hidden = copy_out(kept)
    widened = kept.astype(F32)
    total_sq = group_sum(squares)
    next_normed = (
        widened * lax.rsqrt(total_sq / total_width + EPS) * next_norm_gain[:, None]
    ).astype(BF16)

    return (new_hidden.T, next_normed.T, kv_cache)


def solution(mesh):
    split = Mesh(mesh.devices.reshape(4, 4, 4, 2), ("z", "y", "x", "c"))
    tokens = P(REQ, MLP)
    return jax.shard_map(
        body,
        mesh=split,
        in_specs=(
            tokens, tokens, tokens, tokens, P(REQ), P(REQ, None), tokens, tokens, P(REQ, None),
            P(REQ, None), tokens, P(MLP), P(MLP), P(MLP), P(MLP, None), P(MLP, None), P(), tokens,
            tokens, P(MLP, REQ), P(MLP),
        ),
        out_specs=(tokens, tokens, P(None, MLP, REQ, None)),
        check_vma=False,
    )
```
